512 devices in a mesh: dp: 64 (over z, y_hi, x), shard: 8 (over y_lo, core).
Axes of the slice: x: 4, y: 8 (y_hi: 2, y_lo: 4; y = y_hi * 4 + y_lo), z: 8, core: 2. Of those that a mesh axis runs over, the one named last changes fastest.
Arguments:
- inputs: bfloat16 [512, 8, 8, 8, 256], P(('dp', 'shard')), may hold values from -24 to 24
- cotangent: bfloat16 [512, 4, 4, 4, 256], P(('dp', 'shard')), may hold values from -6 to 6
- weights: bfloat16 [28, 256, 256], P(None, 'shard'), may hold values from -0.078125 to 0.078125
Outputs:
- outputs: bfloat16 [512, 4, 4, 4, 256], P(('dp', 'shard'))
- input_grad: bfloat16 [512, 8, 8, 8, 256], P(('dp', 'shard'))
- weight_grad: float32 [28, 256, 256], P(None, 'shard')
The draws below stay inside these ranges and needn't reach their ends.
All inputs are finite; a program needn't handle non-finite values.
Results may differ from the reference program's by a relative error of at most 0.012.
Values may be sent and summed in bfloat16 or wider, within the bound.
A program may use at most 64 MiB of HBM per device.

```python
import jax
import jax.numpy as jnp
from jax import lax

C = 256
TAPS = 28
P_SIZE = 8
Q = 4
SAMPLES = 512


def strengthened(array, rng, source, target, shards_of, factor):
    owner, partner = [(jnp.arange(array.shape[position]) // (array.shape[position] // shards_of)).reshape([-1 if axis == position else 1 for axis in range(array.ndim)]) for position in (source, target)]
    chosen = jax.random.permutation(rng, shards_of)[partner]
    strong = (owner == chosen) | (owner == (partner + shards_of // 2) % shards_of)
    return jnp.where(strong, factor * array, array)


def steps_of(own_key, dims, cuts, smallest, high):
    def one(position, blocks):
        heights = jax.random.uniform(jax.random.fold_in(jax.random.fold_in(own_key, 6), position), (blocks,), jnp.float32, smallest / len(cuts), high / len(cuts))
        return jnp.repeat(jnp.exp(heights), dims[position] // blocks).reshape((-1,) + (1,) * (len(dims) - position - 1))

    loudness = one(*cuts[0])
    for cut in cuts[1:]:
        loudness = loudness * one(*cut)
    return loudness


def normal_values(rng, extent, deviation, limit, split=(), held_as=jnp.bfloat16):
    gain = steps_of(rng, extent, split, -0.22, 0.18) if split else 1.0
    entries = jax.random.normal(rng, extent, jnp.float32) * deviation * gain
    return jnp.minimum(jnp.maximum(entries, -limit), limit).astype(held_as)


def gaussian_with(own_key, extent, spread, bound, split, heavy, held_as=jnp.bfloat16):
    array = spread * jax.random.normal(own_key, extent, jnp.float32)
    if split:
        array = array * steps_of(own_key, extent, split, -0.22, 0.18)
    return jnp.clip(strengthened(array, jax.random.fold_in(own_key, 3), *heavy), -bound, bound).astype(held_as)


def setup_inputs(seed: int = 0) -> dict:
    arg_keys = jax.random.split(jax.random.key(seed), 4)
    inputs = gaussian_with(arg_keys[0], (SAMPLES, P_SIZE, P_SIZE, P_SIZE, C), 1.0, 24.0, ((0, 512),), (0, 4, 256, 6.0))
    cotangent = normal_values(arg_keys[1], (SAMPLES, Q, Q, Q, C), 1.0, 6.0, ((0, 512),))
    weights = normal_values(arg_keys[2], (TAPS, C, C), (27 * C) ** -0.5, 0.078125, ((1, 8),))
    return {"inputs": inputs, "cotangent": cotangent, "weights": weights}


def one_sample(inputs, cotangent, flat_weights):
    edge = inputs.shape[0]
    half = edge // 2
    chans = inputs.shape[3]
    act = jax.nn.silu(inputs.astype(jnp.float32)).astype(jnp.bfloat16)
    padded = jnp.pad(act, ((1, 1), (1, 1), (1, 1), (0, 0)))
    pieces = []
    for first in range(3):
        for second in range(3):
            for third in range(3):
                pieces.append(padded[first:first + 2 * half:2, second:second + 2 * half:2, third:third + 2 * half:2])
    pieces.append(inputs[0::2, 0::2, 0::2])
    cols = jnp.stack(pieces, axis=3).reshape(half * half * half, 28 * chans)
    outputs = jnp.dot(cols, flat_weights, preferred_element_type=jnp.float32).astype(jnp.bfloat16)
    grad_rows = cotangent.reshape(half * half * half, chans)
    dcols = jnp.dot(grad_rows, flat_weights.T, preferred_element_type=jnp.float32).reshape(half, half, half, 28, chans)
    grid = jnp.zeros((edge + 2, edge + 2, edge + 2, chans), jnp.float32)
    for first in range(3):
        for second in range(3):
            for third in range(3):
                grid = grid.at[first:first + 2 * half:2, second:second + 2 * half:2, third:third + 2 * half:2].add(dcols[:, :, :, 9 * first + 3 * second + third])
    values = inputs.astype(jnp.float32)
    sigma = jax.nn.sigmoid(values)
    grad_in = grid[1:-1, 1:-1, 1:-1] * sigma * (1.0 + values * (1.0 - sigma))
    grad_in = grad_in.at[0::2, 0::2, 0::2].add(dcols[:, :, :, 27])
    sample_grad = jnp.dot(cols.T, grad_rows, preferred_element_type=jnp.float32).astype(jnp.bfloat16)
    return outputs.reshape(half, half, half, chans), grad_in.astype(jnp.bfloat16), sample_grad


def reference(inputs, cotangent, weights):
    flat_weights = weights.reshape(TAPS * C, C)

    def step(total, pair):
        outputs, grad_in, sample_grad = one_sample(pair[0], pair[1], flat_weights)
        return total + sample_grad.astype(jnp.float32), (outputs, grad_in)

    start = jnp.zeros((TAPS * C, C), jnp.float32)
    total, (outputs, input_grad) = lax.scan(step, start, (inputs, cotangent))
    return outputs, input_grad, total.reshape(TAPS, C, C)
```

```python
import functools

import jax
import jax.numpy as jnp
from jax import lax
from jax.experimental import pallas as pl
from jax.experimental.pallas import tpu as pltpu
from jax.sharding import PartitionSpec as P

F32 = jnp.float32
BF16 = jnp.bfloat16
MESH = pl.DeviceIdType.MESH

COMBOS = [(si, sj, sk) for si in (0, -1) for sj in (0, -1) for sk in (0, -1)]
DIRECT = 2


def lane_of(combo):
    return (256 * combo, 256) if combo < 4 else (1024 + 128 * (combo - 4), 128)


def tap_of(combo, parity):
    total = 0
    for weight, shift, odd in zip((9, 3, 1), COMBOS[combo], parity):
        if shift and not odd:
            return None
        total += weight * (1 if not odd else 0 if shift else 2)
    return total


PARITIES = [(a, b, c) for a in (0, 1) for b in (0, 1) for c in (0, 1)]


def dot(a, b, dims):
    return lax.dot_general(a, b, (dims, ((), ())), preferred_element_type=F32)


NN = ((1,), (0,))
NT = ((1,), (1,))
TN = ((0,), (0,))


def one_hot(hit):
    return jnp.where(hit, 1.0, 0.0).astype(BF16)


def sort_target(rows):
    k, j, i = rows & 3, (rows >> 2) & 3, (rows >> 4) & 1
    pk, pj, pi = (rows >> 5) & 1, (rows >> 6) & 1, (rows >> 7) & 1
    return (2 * i + pi) * 64 + (2 * j + pj) * 8 + 2 * k + pk


def kernel(nx, nz, x_hbm, g_hbm, w_hbm, out_hbm, ig_hbm, wg_hbm,
           x_in, g_in, w_in, sortm, sortmt, shiftm, shiftmt, sorted_x, send_x,
           recv_x, recv_g, cols, gcols, wf, wcat, w27, dsilu, gact, send_o, recv_o, own_o,
           send_i, recv_i, out_v, ig_v, gsend, g1, s2, r2, fin,
           in_sem, out_sem, xs, xr, gs, gr, os_, or_, is_, ir, s1s, s1r, s2s, s2r,
           s3s, s3r, s4s, s4r):
    nq = 2 * nz
    taps_x = 28 // nx
    rows_x = taps_x * 32
    rows_q = s2.shape[1]
    dp = lax.axis_index("dp")
    shard = lax.axis_index("shard")
    px = lax.rem(dp, nx)
    y_hi = lax.rem(lax.div(dp, nx), 2)
    pz = lax.div(dp, 2 * nx)
    y = y_hi * 4 + lax.div(shard, 2)
    core = lax.rem(shard, 2)
    sign = 1 - 2 * core
    q = pz * 2 + y_hi

    def at(pz_, y_, px_, core_):
        y_ = lax.rem(y_ + 8, 8)
        return ((pz_ * 2 + lax.div(y_, 4)) * nx + px_, lax.rem(y_, 4) * 2 + core_)

    def slice_of(y_, core_):
        return lax.rem(y_ + 8, 4) * 2 + core_

    def x_peer(d):
        return at(pz, y, lax.rem(px + d, nx), core)

    def q_peer(d):
        other = lax.rem(q + d, nq)
        return at(lax.div(other, 2), lax.rem(other, 2) * 4 + lax.rem(y, 4), px, core)

    def copy(src, dst, send, recv, dev):
        return pltpu.make_async_remote_copy(
            src_ref=src, dst_ref=dst, send_sem=send, recv_sem=recv, device_id=dev, device_id_type=MESH)

    loads = [pltpu.make_async_copy(a, b, in_sem.at[n]) for n, (a, b) in enumerate(((x_hbm, x_in), (g_hbm, g_in), (w_hbm, w_in)))]
    for load in loads:
        load.start()

    peers = [at(pz, y, px, 1 - core)]
    for d in (1, -1):
        for c in (0, 1):
            peers.append(at(pz, y + d, px, c))
    peers += [at(pz, y + 2 * sign, px, core), at(pz, y + 2 * sign, px, 1 - core), at(pz, y - 2 * sign, px, core)]
    peers += [x_peer(d) for d in range(1, nx)]
    peers += [q_peer(d) for d in range(1, nq)]
    barrier = pltpu.get_barrier_semaphore()
    for peer in peers:
        pl.semaphore_signal(barrier, inc=1, device_id=peer, device_id_type=MESH)

    row = lax.broadcasted_iota(jnp.int32, (256, 256), 0)
    col = lax.broadcasted_iota(jnp.int32, (256, 256), 1)
    sortm[...] = one_hot(sort_target(row) == col)
    loads[0].wait()
    for b in range(2):
        got = dot(sortm[...], x_in[b * 256:b * 256 + 256, :], NN)
        for par in range(8):
            sorted_x[par, b * 32:b * 32 + 32, :] = got[par * 32:par * 32 + 32, :]
    for p in range(8):
        for h in range(2):
            send_x[p, :, h * 128:h * 128 + 128] = jnp.concatenate(
                [sorted_x[4 * h + n, :, p * 32:p * 32 + 32] for n in range(4)], axis=1).astype(BF16)
    loads[1].wait()
    pl.semaphore_wait(barrier, len(peers))

    def far(c):
        return 2 - 4 * c

    def to_chip(k):
        return (y, y + 1, y - 1, y + 2 * sign)[k]

    sends = []
    for k in (3, 1, 2, 0):
        for e in (0, 1):
            if k == 0 and e == 0:
                continue
            c = lax.rem(core + e, 2)
            n = 2 * k + e
            dev = at(pz, to_chip(k), px, c)
            slot = 2 * k + core
            sends.append(copy(send_x.at[slice_of(to_chip(k), c)], recv_x.at[slot], xs.at[n], xr.at[slot], dev))
            sends.append(copy(g_in, recv_g.at[slot], gs.at[n], gr.at[slot], dev))
    for send in sends:
        send.start()
    recv_x[core] = send_x[shard]
    recv_g[core] = g_in[...]

    sortmt[...] = one_hot(sort_target(col) == row)
    ri, rj, rk = (row >> 4) & 3, (row >> 2) & 3, row & 3
    ci, cj, ck = (col >> 4) & 3, (col >> 2) & 3, col & 3
    for n, (si, sj, sk) in enumerate(COMBOS):
        if n == 0:
            continue
        step = 16 * si + 4 * sj + sk
        ok = (col == row + step) & (ri >= -si) & (rj >= -sj) & (rk >= -sk)
        shiftm[n] = one_hot(ok)
        ok = (row == col + step) & (ci >= -si) & (cj >= -sj) & (ck >= -sk)
        shiftmt[n] = one_hot(ok)
    wf[...] = jnp.zeros_like(wf)
    wcat[...] = jnp.zeros_like(wcat)
    w27[...] = jnp.zeros_like(w27)
    loads[2].wait()
    for n in range(8):
        first, width = lane_of(n)
        for par, parity in enumerate(PARITIES):
            tap = tap_of(n, parity)
            if tap is None:
                continue
            at_row = first + par * 32 - (256 - width)
            wf[at_row:at_row + 32, :] = w_in[tap]
            wcat[par * 32:par * 32 + 32, n * 256:n * 256 + 256] = w_in[tap]
    first = lane_of(DIRECT)[0]
    wf[first:first + 32, :] = w_in[27]
    w27[0:32, :] = w_in[27]

    def arrived(k, s):
        slot = 2 * k + s
        for buf, sem in ((recv_x, xr), (recv_g, gr)):
            copy(buf.at[slot], buf.at[slot], xs.at[0], sem.at[slot], at(pz, y, px, 1 - core)).wait_recv()

    for half in range(2):
        rows = slice(half * 256, half * 256 + 256)
        if half == 0:
            arrived(0, 1 - core)
            arrived(1, 0)
            arrived(1, 1)
        else:
            for k in (2, 3):
                arrived(k, 0)
                arrived(k, 1)
        raw = recv_x[4 * half:4 * half + 4].reshape(256, 256)
        v = raw.astype(F32)
        s = 1.0 / (1.0 + jnp.exp(-v))
        act = (v * s).astype(BF16)
        dsilu[rows, :] = s * (1.0 + v * (1.0 - s))
        cols[rows, 0:256] = act
        lane = lax.broadcasted_iota(jnp.int32, (256, 256), 1)
        for n in range(1, 8):
            first, width = lane_of(n)
            moved = dot(shiftm[n], act[:, 256 - width:], NN)
            if n == DIRECT:
                moved = jnp.where(lane < 32, v, moved)
            cols[rows, first:first + width] = moved.astype(BF16)

    grads = recv_g[...].reshape(512, 256)
    for block in range(6):
        got = dot(cols[:, block * 256:block * 256 + 256], grads, TN).astype(BF16)
        for n in range(8):
            first, width = lane_of(n)
            if first // 256 != block:
                continue
            for par, parity in enumerate(PARITIES):
                tap = tap_of(n, parity)
                if n == DIRECT and par == 0:
                    tap = 27
                if tap is None:
                    continue
                start = first + par * 32 - (256 - width) - block * 256
                place = (tap % taps_x) * 32
                gsend[tap // taps_x, place:place + 32, :] = got[start:start + 32, :]
    step1 = []
    for d in range(1, nx):
        other = lax.rem(px + d, nx)
        step1.append(copy(gsend.at[other], g1.at[d - 1], s1s.at[d - 1], s1r.at[d - 1], x_peer(d)))
    for send in step1:
        send.start()

    gcols[:, 0:256] = grads
    for half in range(2):
        rows = slice(half * 256, half * 256 + 256)
        for n in range(1, 8):
            gcols[rows, n * 256:n * 256 + 256] = dot(shiftmt[n], grads[rows, :], NN).astype(BF16)
    for half in range(2):
        rows = slice(half * 256, half * 256 + 256)
        got = dot(gcols[rows, :], wcat[...], NT) * dsilu[rows, :]
        direct = dot(grads[rows, :], w27[...], NT)
        for n in range(4):
            one = got[n * 64:n * 64 + 64, :]
            slot = 4 * half + n
            send_i[slot, :, 0:128] = (one[:, 0:128] + direct[n * 64:n * 64 + 64, :]).astype(BF16)
            send_i[slot, :, 128:256] = one[:, 128:256].astype(BF16)
        got = dot(cols[rows, :], wf[...], NN)
        gact[rows, :] = got
        for n in range(4):
            send_o[4 * half + n] = got[n * 64:n * 64 + 64, :].astype(BF16)
    home = []
    for k in (3, 1, 2, 0):
        for e in (0, 1):
            if k == 0 and e == 0:
                continue
            s = e if k else 1 - core
            chip = (y, y - 1, y + 1, y - far(e))[k]
            slot = 2 * k + s
            dev = at(pz, chip, px, s)
            n = 2 * k + e
            home.append(copy(send_i.at[slot], recv_i.at[shard], is_.at[n], ir.at[shard], dev))
            home.append(copy(send_o.at[slot], recv_o.at[shard], os_.at[n], or_.at[shard], dev))
    for send in home:
        send.start()
    recv_i[shard] = send_i[core]
    recv_o[shard] = send_o[core]

    for d in range(1, nx):
        step1[d - 1].wait()
    total = gsend[px].astype(F32)
    for d in range(1, nx):
        total = total + g1[d - 1].astype(F32)
    flat = s2.shape[0] * rows_q
    padded = total.astype(BF16)
    if flat > rows_x:
        padded = jnp.concatenate([padded, jnp.zeros((flat - rows_x, 256), BF16)], axis=0)
    for n in range(nq):
        s2[n] = padded[n * rows_q:n * rows_q + rows_q, :]
    step2 = []
    for d in range(1, nq):
        other = lax.rem(q + d, nq)
        step2.append(copy(s2.at[other], r2.at[d - 1], s2s.at[d - 1], s2r.at[d - 1], q_peer(d)))
    for send in step2:
        send.start()

    for e in range(1, 8):
        slot = lax.rem(shard + e, 8)
        for buf, ssem, sem in ((recv_i, is_, ir), (recv_o, os_, or_)):
            copy(buf.at[slot], buf.at[slot], ssem.at[0], sem.at[slot], at(pz, y, px, 1 - core)).wait_recv()
    out_v[...] = jnp.sum(recv_o[...].astype(F32), axis=0).astype(BF16)
    for par in range(8):
        for h in range(2):
            sorted_x[par, :, h * 128:h * 128 + 128] = jnp.concatenate(
                [recv_i[4 * h + n, :, par * 32:par * 32 + 32].astype(F32) for n in range(4)], axis=1)
    for b in range(2):
        natural = sorted_x[:, b * 32:b * 32 + 32, :].reshape(256, 256).astype(BF16)
        ig_v[b * 256:b * 256 + 256, :] = dot(sortmt[...], natural, NN).astype(BF16)
    stores = [pltpu.make_async_copy(out_v, out_hbm, out_sem.at[0]), pltpu.make_async_copy(ig_v, ig_hbm, out_sem.at[1])]
    for store in stores:
        store.start()

    for send in step2:
        send.wait()
    chunk = s2[q].astype(F32)
    for d in range(1, nq):
        chunk = chunk + r2[d - 1].astype(F32)
    mine = pl.ds(pl.multiple_of(q * rows_q, 16), rows_q)
    fin[px, mine, :] = chunk.astype(BF16)

    step3 = []
    for d in range(1, nq):
        step3.append(copy(fin.at[px, mine], fin.at[px, mine], s3s.at[d - 1], s3r.at[d - 1], q_peer(d)))
    for send in step3:
        send.start()
    for d in range(1, nq):
        other = lax.rem(q + nq - d, nq)
        theirs = pl.ds(pl.multiple_of(other * rows_q, 16), rows_q)
        copy(fin.at[px, theirs], fin.at[px, theirs], s3s.at[d - 1], s3r.at[d - 1], q_peer(d)).wait_recv()
    part = pl.ds(0, rows_x)
    step4 = []
    for d in range(1, nx):
        step4.append(copy(fin.at[px, part], fin.at[px, part], s4s.at[d - 1], s4r.at[d - 1], x_peer(d)))
    for send in step4:
        send.start()
    for d in range(1, nx):
        other = lax.rem(px + nx - d, nx)
        copy(fin.at[other, part], fin.at[other, part], s4s.at[d - 1], s4r.at[d - 1], x_peer(d)).wait_recv()
    last = pltpu.make_async_copy(fin.at[:, part], wg_hbm, out_sem.at[2])
    last.start()

    for send in sends + home + step3 + step4:
        send.wait_send()
    for store in stores:
        store.wait()
    last.wait()


def shards(nx, nz, inputs, cotangent, weights):
    nq = 2 * nz
    rows_x = 28 // nx * 32
    rows_q = -(-rows_x // nq // 16) * 16
    sems = [pltpu.SemaphoreType.DMA((n,)) for n in (3, 3, 8, 8, 8, 8, 8, 8, 8, 8)]
    sems += [pltpu.SemaphoreType.DMA((max(n - 1, 1),)) for n in (nx, nx, nq, nq, nq, nq, nx, nx)]
    vm = pltpu.VMEM
    scratch = [
        vm((512, 256), BF16), vm((64, 256), BF16), vm((28, 32, 256), BF16),
        vm((256, 256), BF16), vm((256, 256), BF16), vm((8, 256, 256), BF16), vm((8, 256, 256), BF16),
        vm((8, 64, 256), F32), vm((8, 64, 256), BF16),
        vm((8, 64, 256), BF16), vm((8, 64, 256), BF16),
        vm((512, 1536), BF16), vm((512, 2048), BF16),
        vm((1536, 256), BF16), vm((256, 2048), BF16), vm((128, 256), BF16),
        vm((512, 256), F32), vm((512, 256), F32),
        vm((8, 64, 256), BF16), vm((8, 64, 256), BF16), vm((64, 256), F32),
        vm((8, 64, 256), BF16), vm((8, 64, 256), BF16),
        vm((64, 256), BF16), vm((512, 256), BF16),
        vm((nx, rows_x, 256), BF16), vm((max(nx - 1, 1), rows_x, 256), BF16),
        vm((nq, rows_q, 256), BF16), vm((nq - 1, rows_q, 256), BF16),
        vm((nx, nq * rows_q, 256), BF16),
    ] + sems
    hbm = pl.BlockSpec(memory_space=pl.ANY)
    out, ig, wg = pl.pallas_call(
        functools.partial(kernel, nx, nz),
        out_shape=(
            jax.ShapeDtypeStruct((64, 256), BF16),
            jax.ShapeDtypeStruct((512, 256), BF16),
            jax.ShapeDtypeStruct((nx, rows_x, 256), BF16),
        ),
        in_specs=[hbm] * 3,
        out_specs=(hbm,) * 3,
        scratch_shapes=scratch,
        compiler_params=pltpu.CompilerParams(
            collective_id=0, has_side_effects=True, vmem_limit_bytes=48 * 2**20),
        name="unit",
    )(inputs.reshape(512, 256), cotangent.reshape(64, 256), weights)
    return (
        out.reshape(1, 4, 4, 4, 256),
        ig.reshape(1, 8, 8, 8, 256),
        wg.reshape(28, 32, 256).astype(F32),
    )


def solution(mesh, nx=4):
    nz = mesh.shape["dp"] // (2 * nx)
    rows = P(("dp", "shard"), None, None, None, None)
    return jax.shard_map(
        functools.partial(shards, nx, nz),
        mesh=mesh,
        in_specs=(rows, rows, P(None, "shard", None)),
        out_specs=(rows, rows, P(None, "shard", None)),
        check_vma=False,
    )
```

```python
import functools

import jax
import jax.numpy as jnp
from jax import lax
from jax.experimental import pallas as pl
from jax.experimental.pallas import tpu as pltpu
from jax.sharding import PartitionSpec as P

F32 = jnp.float32
BF16 = jnp.bfloat16
MESH = pl.DeviceIdType.MESH

COMBOS = [(si, sj, sk) for si in (0, -1) for sj in (0, -1) for sk in (0, -1)]
DIRECT = 2


def lane_of(combo):
    return (256 * combo, 256) if combo < 4 else (1024 + 128 * (combo - 4), 128)


def tap_of(combo, parity):
    total = 0
    for weight, shift, odd in zip((9, 3, 1), COMBOS[combo], parity):
        if shift and not odd:
            return None
        total += weight * (1 if not odd else 0 if shift else 2)
    return total


PARITIES = [(a, b, c) for a in (0, 1) for b in (0, 1) for c in (0, 1)]


def dot(a, b, dims):
    return lax.dot_general(a, b, (dims, ((), ())), preferred_element_type=F32)


NN = ((1,), (0,))
NT = ((1,), (1,))
TN = ((0,), (0,))


def one_hot(hit):
    return jnp.where(hit, 1.0, 0.0).astype(BF16)


def sort_target(rows):
    k, j, i = rows & 3, (rows >> 2) & 3, (rows >> 4) & 1
    pk, pj, pi = (rows >> 5) & 1, (rows >> 6) & 1, (rows >> 7) & 1
    return (2 * i + pi) * 64 + (2 * j + pj) * 8 + 2 * k + pk


def kernel(nx, nz, x_hbm, g_hbm, w_hbm, out_v, ig_v, fin,
           x_in, g_raw, g_in, w_in, sortm, sortmt, shiftm, shiftmt, sorted_x, send_x,
           recv_x, recv_g, cols, gcols, wf, wcat, w27, dsilu, send_o, recv_o,
           send_i, recv_i, gsend, g1, s2, r2,
           in_sem, xs, xr, gs, gr, fs, os_, or_, is_, ir, s1s, s1r, s2s, s2r,
           s3s, s3r, s4s, s4r, near, middle, across):
    nq = 2 * nz
    quads = 2 if nz > 1 else 1
    size = nz // quads
    taps_x = 28 // nx
    rows_q = s2.shape[1]
    rows_g = size * rows_q
    dp = lax.axis_index("dp")
    shard = lax.axis_index("shard")
    px = lax.rem(dp, nx)
    y_hi = lax.rem(lax.div(dp, nx), 2)
    pz = lax.div(dp, 2 * nx)
    y = y_hi * 4 + lax.div(shard, 2)
    core = lax.rem(shard, 2)
    sign = 1 - 2 * core
    q = y_hi * nz + pz

    def at(pz_, y_, px_, core_):
        y_ = lax.rem(y_ + 8, 8)
        return ((pz_ * 2 + lax.div(y_, 4)) * nx + px_, lax.rem(y_, 4) * 2 + core_)

    def slice_of(y_, core_):
        return lax.rem(y_ + 8, 4) * 2 + core_

    def x_peer(d):
        return at(pz, y, lax.rem(px + d, nx), core)

    def z_peer(d):
        return at(lax.rem(pz + d + nz, nz), y, px, core)

    def owner(other):
        return at(lax.rem(other, nz), lax.div(other, nz) * 4 + lax.rem(y, 4), px, core)

    partner = at(pz, y, px, 1 - core)

    def copy(src, dst, send, recv, dev):
        return pltpu.make_async_remote_copy(
            src_ref=src, dst_ref=dst, send_sem=send, recv_sem=recv, device_id=dev, device_id_type=MESH)

    def signal(sem, dev):
        pl.semaphore_signal(sem, inc=1, device_id=dev, device_id_type=MESH)

    loads = [pltpu.make_async_copy(a, b, in_sem.at[n]) for n, (a, b) in enumerate(((x_hbm, x_in), (g_hbm, g_raw), (w_hbm, w_in)))]
    for load in loads:
        load.start()

    peers = [partner]
    for d in (1, -1):
        for c in (0, 1):
            peers.append(at(pz, y + d, px, c))
    peers += [at(pz, y + 2 * sign, px, core), at(pz, y + 2 * sign, px, 1 - core), at(pz, y - 2 * sign, px, core)]
    peers += [x_peer(d) for d in range(1, nx)]
    if nz > 1:
        peers += [z_peer(1), z_peer(-1)]
    barrier = pltpu.get_barrier_semaphore()
    for peer in peers:
        signal(barrier, peer)

    row = lax.broadcasted_iota(jnp.int32, (256, 256), 0)
    col = lax.broadcasted_iota(jnp.int32, (256, 256), 1)
    sortm[...] = one_hot(sort_target(row) == col)
    loads[0].wait()
    for b in range(2):
        got = dot(sortm[...], x_in[b * 256:b * 256 + 256, :], NN)
        for par in range(8):
            sorted_x[par, b * 32:b * 32 + 32, :] = got[par * 32:par * 32 + 32, :]
    for p in range(8):
        for h in range(2):
            send_x[p, :, h * 128:h * 128 + 128] = jnp.concatenate(
                [sorted_x[4 * h + n, :, p * 32:p * 32 + 32] for n in range(4)], axis=1).astype(BF16)
    loads[1].wait()
    g_in[...] = g_raw[...].astype(F32).reshape(64, 256).astype(BF16)
    pl.semaphore_wait(barrier, len(peers))

    def far(c):
        return 2 - 4 * c

    def to_chip(k):
        return (y, y + 1, y - 1, y + 2 * sign)[k]

    sends = []
    for k in (3, 1, 2):
        slot = 2 * k + core
        sends.append(copy(g_in, recv_g.at[slot], gs.at[k], gr.at[slot], at(pz, to_chip(k), px, core)))
    sends.append(copy(g_in, recv_g.at[core], gs.at[0], gr.at[core], partner))
    for k in (3, 1, 2, 0):
        for e in (0, 1):
            if k == 0 and e == 0:
                continue
            c = lax.rem(core + e, 2)
            slot = 2 * k + core
            sends.append(copy(send_x.at[slice_of(to_chip(k), c)], recv_x.at[slot], xs.at[2 * k + e], xr.at[slot],
                              at(pz, to_chip(k), px, c)))
    for send in sends:
        send.start()
    if nz > 1:
        signal(near, z_peer(1))
        signal(near, z_peer(-1))
    recv_x[core] = send_x[shard]
    recv_g[core] = g_in[...]

    sortmt[...] = one_hot(sort_target(col) == row)
    ri, rj, rk = (row >> 4) & 3, (row >> 2) & 3, row & 3
    ci, cj, ck = (col >> 4) & 3, (col >> 2) & 3, col & 3
    for n, (si, sj, sk) in enumerate(COMBOS):
        if n == 0:
            continue
        step = 16 * si + 4 * sj + sk
        ok = (col == row + step) & (ri >= -si) & (rj >= -sj) & (rk >= -sk)
        shiftm[n] = one_hot(ok)
        ok = (row == col + step) & (ci >= -si) & (cj >= -sj) & (ck >= -sk)
        shiftmt[n] = one_hot(ok)
    wf[...] = jnp.zeros_like(wf)
    wcat[...] = jnp.zeros_like(wcat)
    w27[...] = jnp.zeros_like(w27)
    loads[2].wait()
    for n in range(8):
        first, width = lane_of(n)
        for par, parity in enumerate(PARITIES):
            tap = tap_of(n, parity)
            if tap is None:
                continue
            at_row = first + par * 32 - (256 - width)
            wf[at_row:at_row + 32, :] = w_in[tap]
            wcat[par * 32:par * 32 + 32, n * 256:n * 256 + 256] = w_in[tap]
    first = lane_of(DIRECT)[0]
    wf[first:first + 32, :] = w_in[27]
    w27[0:32, :] = w_in[27]

    if nz > 1:
        pl.semaphore_wait(near, 2)
        signal(middle, z_peer(2))
        signal(middle, z_peer(-2))

    def arrived(buf, sem, slot):
        copy(buf.at[slot], buf.at[slot], xs.at[0], sem.at[slot], partner).wait_recv()

    for k in (1, 2, 3):
        slot = 2 * k + core
        arrived(recv_g, gr, slot)
        sends.append(copy(recv_g.at[slot], recv_g.at[slot], fs.at[k], gr.at[slot], partner))
        sends[-1].start()

    for half in range(2):
        rows = slice(half * 256, half * 256 + 256)
        for k in (2 * half, 2 * half + 1):
            for e in (0, 1):
                if k or e:
                    arrived(recv_x, xr, 2 * k + lax.rem(core + e, 2))
        raw = recv_x[4 * half:4 * half + 4].reshape(256, 256)
        v = raw.astype(F32)
        s = 1.0 / (1.0 + jnp.exp(-v))
        act = (v * s).astype(BF16)
        dsilu[rows, :] = s * (1.0 + v * (1.0 - s))
        cols[rows, 0:256] = act
        lane = lax.broadcasted_iota(jnp.int32, (256, 256), 1)
        for n in range(1, 8):
            first, width = lane_of(n)
            moved = dot(shiftm[n], act[:, 256 - width:], NN)
            if n == DIRECT:
                moved = jnp.where(lane < 32, v, moved)
            cols[rows, first:first + width] = moved.astype(BF16)

    for k in range(4):
        arrived(recv_g, gr, 2 * k + 1 - core)
    if nz > 1:
        pl.semaphore_wait(middle, 2)
    signal(across, at(pz, y + 4, px, core))

    grads = recv_g[...].reshape(512, 256)
    for block in range(6):
        got = dot(cols[:, block * 256:block * 256 + 256], grads, TN).astype(BF16)
        for n in range(8):
            first, width = lane_of(n)
            if first // 256 != block:
                continue
            for par, parity in enumerate(PARITIES):
                tap = tap_of(n, parity)
                if n == DIRECT and par == 0:
                    tap = 27
                if tap is None:
                    continue
                start = first + par * 32 - (256 - width) - block * 256
                place = (tap % taps_x) * 32
                gsend[tap // taps_x, place:place + 32, :] = got[start:start + 32, :]
    if rows_g * 2 * quads > taps_x * 32:
        gsend[:, taps_x * 32:, :] = jnp.zeros((nx, rows_g * 2 * quads - taps_x * 32, 256), BF16)
    zq = lax.div(pz, size)
    groups = [(1 - y_hi) * quads + quads - 1 - zq, (1 - y_hi) * quads + zq, y_hi * quads + quads - 1 - zq, y_hi * quads + zq]
    if quads == 1:
        groups = groups[1::2]
    ng = len(groups)
    parts = [pl.ds(pl.multiple_of(g * rows_g, 16), rows_g) for g in groups]
    step1 = []
    for r in range(ng):
        for d in range(1, nx):
            other = lax.rem(px + d, nx)
            n = r * (nx - 1) + d - 1
            step1.append(copy(gsend.at[other, parts[r]], g1.at[d - 1, r], s1s.at[n], s1r.at[n], x_peer(d)))
    for send in step1:
        send.start()

    gcols[:, 0:256] = grads
    for half in range(2):
        rows = slice(half * 256, half * 256 + 256)
        for n in range(1, 8):
            gcols[rows, n * 256:n * 256 + 256] = dot(shiftmt[n], grads[rows, :], NN).astype(BF16)
    for half in range(2):
        rows = slice(half * 256, half * 256 + 256)
        got = dot(gcols[rows, :], wcat[...], NT) * dsilu[rows, :]
        direct = dot(grads[rows, :], w27[...], NT)
        for n in range(4):
            one = got[n * 64:n * 64 + 64, :]
            slot = 4 * half + n
            send_i[slot, :, 0:128] = (one[:, 0:128] + direct[n * 64:n * 64 + 64, :]).astype(BF16)
            send_i[slot, :, 128:256] = one[:, 128:256].astype(BF16)
        got = dot(cols[rows, :], wf[...], NN)
        for n in range(4):
            send_o[4 * half + n] = got[n * 64:n * 64 + 64, :].astype(BF16)
    home = []
    for k in (3, 1, 2, 0):
        for e in (0, 1):
            if k == 0 and e == 0:
                continue
            s = e if k else 1 - core
            chip = (y, y - 1, y + 1, y - far(e))[k]
            slot = 2 * k + s
            dev = at(pz, chip, px, s)
            n = 2 * k + e
            home.append(copy(send_i.at[slot], recv_i.at[shard], is_.at[n], ir.at[shard], dev))
            home.append(copy(send_o.at[slot], recv_o.at[shard], os_.at[n], or_.at[shard], dev))
    for send in home:
        send.start()
    recv_i[shard] = send_i[core]
    recv_o[shard] = send_o[core]

    pl.semaphore_wait(across, 1)
    step2 = []
    for r in range(ng):
        for d in range(1, nx):
            step1[r * (nx - 1) + d - 1].wait()
        total = gsend[px, parts[r], :].astype(F32)
        for d in range(1, nx):
            total = total + g1[d - 1, r].astype(F32)
        total = total.astype(BF16)
        for n in range(size):
            s2[groups[r] * size + n] = total[n * rows_q:n * rows_q + rows_q, :]
        for e in range(size - 1, -1, -1):
            if r == ng - 1 and e == 0:
                continue
            other = groups[r] * size + lax.rem(pz + e, size)
            n = r * size + e
            step2.append(copy(s2.at[other], r2.at[q], s2s.at[n], s2r.at[q], owner(other)))
            step2[-1].start()
    r2[q] = s2[q]

    for e in range(1, 8):
        slot = lax.rem(shard + e, 8)
        for buf, ssem, sem in ((recv_i, is_, ir), (recv_o, os_, or_)):
            copy(buf.at[slot], buf.at[slot], ssem.at[0], sem.at[slot], at(pz, y, px, 1 - core)).wait_recv()
    out_v[...] = jnp.sum(recv_o[...].astype(F32), axis=0).astype(BF16)
    for par in range(8):
        for h in range(2):
            sorted_x[par, :, h * 128:h * 128 + 128] = jnp.concatenate(
                [recv_i[4 * h + n, :, par * 32:par * 32 + 32].astype(F32) for n in range(4)], axis=1)
    for b in range(2):
        natural = sorted_x[:, b * 32:b * 32 + 32, :].reshape(256, 256).astype(BF16)
        ig_v[b * 256:b * 256 + 256, :] = dot(sortmt[...], natural, NN).astype(BF16)

    for d in range(1, nq):
        other = lax.rem(q + d, nq)
        copy(r2.at[other], r2.at[other], s2s.at[0], s2r.at[other], partner).wait_recv()
    mine = pl.ds(pl.multiple_of(q * rows_q, 16), rows_q)
    fin[px, mine, :] = jnp.sum(r2[...].astype(F32), axis=0).astype(BF16)

    step3 = []
    for r in range(ng):
        for e in range(size - 1, -1, -1):
            if r == ng - 1 and e == 0:
                continue
            other = groups[r] * size + lax.rem(pz + e, size)
            step3.append(copy(fin.at[px, mine], fin.at[px, mine], s3s.at[r * size + e], s3r.at[q], owner(other)))
            step3[-1].start()
    step4 = []
    for r in range(ng - 1, -1, -1):
        for e in range(size):
            if r == ng - 1 and e == 0:
                continue
            other = groups[r] * size + lax.rem(pz + e, size)
            theirs = pl.ds(pl.multiple_of(other * rows_q, 16), rows_q)
            copy(fin.at[px, theirs], fin.at[px, theirs], s3s.at[0], s3r.at[other], partner).wait_recv()
        for d in range(1, nx):
            n = r * (nx - 1) + d - 1
            step4.append(copy(fin.at[px, parts[r]], fin.at[px, parts[r]], s4s.at[n], s4r.at[n], x_peer(d)))
            step4[-1].start()
    for r in range(ng - 1, -1, -1):
        for d in range(1, nx):
            n = r * (nx - 1) + d - 1
            other = lax.rem(px + nx - d, nx)
            copy(fin.at[other, parts[r]], fin.at[other, parts[r]], s4s.at[n], s4r.at[n], x_peer(d)).wait_recv()
    for send in sends + home + step2 + step3 + step4:
        send.wait_send()


def finish(out_v, ig_v, fin, out_hbm, ig_hbm, wg_hbm, out_s, wg_s, sem):
    nx, rows = wg_s.shape[:2]
    stores = [pltpu.make_async_copy(ig_v, ig_hbm, sem.at[0])]
    stores[0].start()
    for n in range(nx):
        wg_s[n] = fin[n, 0:rows, :].astype(F32)
        stores.append(pltpu.make_async_copy(wg_s.at[n], wg_hbm.at[n], sem.at[n + 1]))
        stores[-1].start()
    out_s[...] = out_v[...].astype(F32).reshape(4, 4, 4, 256).astype(BF16)
    stores.append(pltpu.make_async_copy(out_s, out_hbm, sem.at[nx + 1]))
    stores[-1].start()
    for store in stores:
        store.wait()


def shards(nx, nz, inputs, cotangent, weights):
    nq = 2 * nz
    quads = 2 if nz > 1 else 1
    ng = 2 * quads
    rows_x = 28 // nx * 32
    rows_q = -(-rows_x // nq // 16) * 16
    rows_g = nz // quads * rows_q
    dma = pltpu.SemaphoreType.DMA
    sems = [dma((n,)) for n in (3, 8, 8, 4, 8, 4, 8, 8, 8, 8)]
    sems += [dma((max(n, 1),)) for n in (ng * (nx - 1), ng * (nx - 1), nq, nq, nq, nq, ng * (nx - 1), ng * (nx - 1))]
    sems += [pltpu.SemaphoreType.REGULAR] * 3
    vm = pltpu.VMEM
    scratch = [
        vm((512, 256), BF16), vm((4, 4, 4, 256), BF16), vm((64, 256), BF16), vm((28, 32, 256), BF16),
        vm((256, 256), BF16), vm((256, 256), BF16), vm((8, 256, 256), BF16), vm((8, 256, 256), BF16),
        vm((8, 64, 256), F32), vm((8, 64, 256), BF16),
        vm((8, 64, 256), BF16), vm((8, 64, 256), BF16),
        vm((512, 1536), BF16), vm((512, 2048), BF16),
        vm((1536, 256), BF16), vm((256, 2048), BF16), vm((128, 256), BF16),
        vm((512, 256), F32),
        vm((8, 64, 256), BF16), vm((8, 64, 256), BF16),
        vm((8, 64, 256), BF16), vm((8, 64, 256), BF16),
        vm((nx, ng * rows_g, 256), BF16), vm((max(nx - 1, 1), ng, rows_g, 256), BF16),
        vm((nq, rows_q, 256), BF16), vm((nq, rows_q, 256), BF16),
    ] + sems
    hbm = pl.BlockSpec(memory_space=pltpu.HBM)
    vmem = pl.BlockSpec(memory_space=pltpu.VMEM)
    out, ig, wg = pl.pallas_call(
        functools.partial(kernel, nx, nz),
        out_shape=(
            jax.ShapeDtypeStruct((64, 256), BF16),
            jax.ShapeDtypeStruct((512, 256), BF16),
            jax.ShapeDtypeStruct((nx, ng * rows_g, 256), BF16),
        ),
        in_specs=[hbm] * 3,
        out_specs=(vmem,) * 3,
        scratch_shapes=scratch,
        compiler_params=pltpu.CompilerParams(
            collective_id=0, has_side_effects=True, vmem_limit_bytes=48 * 2**20),
        name="unit",
    )(*[pltpu.with_memory_space_constraint(a, pltpu.HBM)
        for a in (inputs.reshape(512, 256), cotangent.reshape(4, 4, 4, 256), weights)])
    out, ig, wg = pl.pallas_call(
        finish,
        out_shape=(
            jax.ShapeDtypeStruct((4, 4, 4, 256), BF16),
            jax.ShapeDtypeStruct((512, 256), BF16),
            jax.ShapeDtypeStruct((nx, rows_x, 256), F32),
        ),
        in_specs=[vmem] * 3,
        out_specs=(hbm,) * 3,
        scratch_shapes=[vm((4, 4, 4, 256), BF16), vm((nx, rows_x, 256), F32), dma((nx + 2,))],
        compiler_params=pltpu.CompilerParams(vmem_limit_bytes=8 * 2**20),
        name="finish",
    )(out, ig, wg)
    return (
        out.reshape(1, 4, 4, 4, 256),
        ig.reshape(1, 8, 8, 8, 256),
        wg.reshape(28, 32, 256),
    )


def solution(mesh, nx=4):
    nz = mesh.shape["dp"] // (2 * nx)
    rows = P(("dp", "shard"), None, None, None, None)
    return jax.shard_map(
        functools.partial(shards, nx, nz),
        mesh=mesh,
        in_specs=(rows, rows, P(None, "shard", None)),
        out_specs=(rows, rows, P(None, "shard", None)),
        check_vma=False,
    )
```

```python
import functools

import jax
import jax.numpy as jnp
from jax import lax
from jax.experimental import pallas as pl
from jax.experimental.pallas import tpu as pltpu
from jax.sharding import PartitionSpec as P

F32 = jnp.float32
BF16 = jnp.bfloat16
MESH = pl.DeviceIdType.MESH

COMBOS = [(si, sj, sk) for si in (0, -1) for sj in (0, -1) for sk in (0, -1)]
IDLE = 4
DIRECT = 2


def lane_of(combo):
    return (256 * combo, 256) if combo < 4 else (1024 + 128 * (combo - 4), 128)


def tap_of(combo, parity):
    total = 0
    for weight, shift, odd in zip((9, 3, 1), COMBOS[combo], parity):
        if shift and not odd:
            return None
        total += weight * (1 if not odd else 0 if shift else 2)
    return total


PARITIES = [(a, b, c) for a in (0, 1) for b in (0, 1) for c in (0, 1)]


def dot(a, b, dims):
    return lax.dot_general(a, b, (dims, ((), ())), preferred_element_type=F32)


NN = ((1,), (0,))
NT = ((1,), (1,))
TN = ((0,), (0,))


def one_hot(hit):
    return jnp.where(hit, 1.0, 0.0).astype(BF16)


def sort_target(rows):
    k, j, i = rows & 3, (rows >> 2) & 3, (rows >> 4) & 1
    pk, pj, pi = (rows >> 5) & 1, (rows >> 6) & 1, (rows >> 7) & 1
    return (2 * i + pi) * 64 + (2 * j + pj) * 8 + 2 * k + pk


def kernel(nx, nz, x_hbm, g_hbm, w_hbm, out_v, ig_v, fin,
           x_in, g_raw, g_in, w_in, sortm, sortmt, shiftm, shiftmt, sorted_x, send_x,
           recv_x, recv_g, cols, gcols, wf, wcat, w27, dsilu, send_o, recv_o,
           send_i, recv_i, gsend, g1, s2, r2,
           in_sem, xs, xr, gs, gr, fs, os_, or_, is_, ir, s1s, s1r, s2s, s2r,
           s3s, s3r, s4s, s4r, near, middle, across):
    nq = 2 * nz
    taps_x = 28 // nx
    rows_q = s2.shape[1]
    ring = s2.shape[0] // 2
    dp = lax.axis_index("dp")
    shard = lax.axis_index("shard")
    px = lax.rem(dp, nx)
    y_hi = lax.rem(lax.div(dp, nx), 2)
    pz = lax.div(dp, 2 * nx)
    y = y_hi * 4 + lax.div(shard, 2)
    core = lax.rem(shard, 2)
    sign = 1 - 2 * core
    q = y_hi * nz + pz

    def at(pz_, y_, px_, core_):
        y_ = lax.rem(y_ + 8, 8)
        return ((pz_ * 2 + lax.div(y_, 4)) * nx + px_, lax.rem(y_, 4) * 2 + core_)

    def slice_of(y_, core_):
        return lax.rem(y_ + 8, 4) * 2 + core_

    def x_peer(d):
        return at(pz, y, lax.rem(px + d, nx), core)

    def z_peer(d):
        return at(lax.rem(pz + d + nz, nz), y, px, core)

    here = lax.rem(pz - lax.div(pz, IDLE + 1), nz) if ring < nz else pz
    is_owner = pz != IDLE
    mine = y_hi * ring + here

    def owner(y_, n):
        return at(n + lax.div(n, IDLE) if ring < nz else n, y_ * 4 + lax.rem(y, 4), px, core)

    def order():
        offsets = sorted(range(ring), key=lambda e: -min(e, ring - e))
        for other_y in (1, 0):
            for e in offsets:
                y_ = 1 - y_hi if other_y else y_hi
                yield not other_y and e == 0, y_, lax.rem(here + e, ring)

    def piece(n):
        return pl.ds(pl.multiple_of(n * rows_q, 16), rows_q)

    partner = at(pz, y, px, 1 - core)

    def copy(src, dst, send, recv, dev):
        return pltpu.make_async_remote_copy(
            src_ref=src, dst_ref=dst, send_sem=send, recv_sem=recv, device_id=dev, device_id_type=MESH)

    def signal(sem, dev):
        pl.semaphore_signal(sem, inc=1, device_id=dev, device_id_type=MESH)

    loads = [pltpu.make_async_copy(a, b, in_sem.at[n]) for n, (a, b) in enumerate(((x_hbm, x_in), (g_hbm, g_raw), (w_hbm, w_in)))]
    for load in loads:
        load.start()

    peers = [partner]
    for d in (1, -1):
        for c in (0, 1):
            peers.append(at(pz, y + d, px, c))
    peers += [at(pz, y + 2 * sign, px, core), at(pz, y + 2 * sign, px, 1 - core), at(pz, y - 2 * sign, px, core)]
    peers += [x_peer(d) for d in range(1, nx)]
    if nz > 1:
        peers += [z_peer(1), z_peer(-1)]
    barrier = pltpu.get_barrier_semaphore()
    for peer in peers:
        signal(barrier, peer)

    row = lax.broadcasted_iota(jnp.int32, (256, 256), 0)
    col = lax.broadcasted_iota(jnp.int32, (256, 256), 1)
    sortm[...] = one_hot(sort_target(row) == col)
    loads[0].wait()
    for b in range(2):
        got = dot(sortm[...], x_in[b * 256:b * 256 + 256, :], NN)
        for par in range(8):
            sorted_x[par, b * 32:b * 32 + 32, :] = got[par * 32:par * 32 + 32, :]
    for p in range(8):
        for h in range(2):
            send_x[p, :, h * 128:h * 128 + 128] = jnp.concatenate(
                [sorted_x[4 * h + n, :, p * 32:p * 32 + 32] for n in range(4)], axis=1).astype(BF16)
    loads[1].wait()
    g_in[...] = g_raw[...].astype(F32).reshape(64, 256).astype(BF16)
    pl.semaphore_wait(barrier, len(peers))

    def far(c):
        return 2 - 4 * c

    def to_chip(k):
        return (y, y + 1, y - 1, y + 2 * sign)[k]

    sends = []
    for k in (3, 1, 2):
        slot = 2 * k + core
        sends.append(copy(g_in, recv_g.at[slot], gs.at[k], gr.at[slot], at(pz, to_chip(k), px, core)))
    sends.append(copy(g_in, recv_g.at[core], gs.at[0], gr.at[core], partner))
    for k in (3, 1, 2, 0):
        for e in (0, 1):
            if k == 0 and e == 0:
                continue
            c = lax.rem(core + e, 2)
            slot = 2 * k + core
            sends.append(copy(send_x.at[slice_of(to_chip(k), c)], recv_x.at[slot], xs.at[2 * k + e], xr.at[slot],
                              at(pz, to_chip(k), px, c)))
    if nz > 1:
        signal(near, z_peer(1))
        signal(near, z_peer(-1))
    for send in sends:
        send.start()
    recv_x[core] = send_x[shard]
    recv_g[core] = g_in[...]

    sortmt[...] = one_hot(sort_target(col) == row)
    ri, rj, rk = (row >> 4) & 3, (row >> 2) & 3, row & 3
    ci, cj, ck = (col >> 4) & 3, (col >> 2) & 3, col & 3
    for n, (si, sj, sk) in enumerate(COMBOS):
        if n == 0:
            continue
        step = 16 * si + 4 * sj + sk
        ok = (col == row + step) & (ri >= -si) & (rj >= -sj) & (rk >= -sk)
        shiftm[n] = one_hot(ok)
        ok = (row == col + step) & (ci >= -si) & (cj >= -sj) & (ck >= -sk)
        shiftmt[n] = one_hot(ok)
    wf[...] = jnp.zeros_like(wf)
    wcat[...] = jnp.zeros_like(wcat)
    w27[...] = jnp.zeros_like(w27)
    loads[2].wait()
    for n in range(8):
        first, width = lane_of(n)
        for par, parity in enumerate(PARITIES):
            tap = tap_of(n, parity)
            if tap is None:
                continue
            at_row = first + par * 32 - (256 - width)
            wf[at_row:at_row + 32, :] = w_in[tap]
            wcat[par * 32:par * 32 + 32, n * 256:n * 256 + 256] = w_in[tap]
    first = lane_of(DIRECT)[0]
    wf[first:first + 32, :] = w_in[27]
    w27[0:32, :] = w_in[27]

    def arrived(buf, sem, slot):
        copy(buf.at[slot], buf.at[slot], xs.at[0], sem.at[slot], partner).wait_recv()

    for k in (1, 2, 3):
        slot = 2 * k + core
        arrived(recv_g, gr, slot)
        sends.append(copy(recv_g.at[slot], recv_g.at[slot], fs.at[k], gr.at[slot], partner))
        sends[-1].start()

    for half in range(2):
        rows = slice(half * 256, half * 256 + 256)
        if nz > 1 and half == 1:
            pl.semaphore_wait(near, 2)
            signal(middle, z_peer(2))
            signal(middle, z_peer(-2))
        for k in (2 * half, 2 * half + 1):
            for e in (0, 1):
                if k or e:
                    arrived(recv_x, xr, 2 * k + lax.rem(core + e, 2))
        raw = recv_x[4 * half:4 * half + 4].reshape(256, 256)
        v = raw.astype(F32)
        s = 1.0 / (1.0 + jnp.exp(-v))
        act = (v * s).astype(BF16)
        dsilu[rows, :] = s * (1.0 + v * (1.0 - s))
        cols[rows, 0:256] = act
        lane = lax.broadcasted_iota(jnp.int32, (256, 256), 1)
        for n in range(1, 8):
            first, width = lane_of(n)
            moved = dot(shiftm[n], act[:, 256 - width:], NN)
            if n == DIRECT:
                moved = jnp.where(lane < 32, v, moved)
            cols[rows, first:first + width] = moved.astype(BF16)

    for k in range(4):
        arrived(recv_g, gr, 2 * k + 1 - core)
    if nz > 1:
        pl.semaphore_wait(middle, 2)
    signal(across, at(pz, y + 4, px, core))

    grads = recv_g[...].reshape(512, 256)
    for block in range(6):
        got = dot(cols[:, block * 256:block * 256 + 256], grads, TN).astype(BF16)
        for n in range(8):
            first, width = lane_of(n)
            if first // 256 != block:
                continue
            for par, parity in enumerate(PARITIES):
                tap = tap_of(n, parity)
                if n == DIRECT and par == 0:
                    tap = 27
                if tap is None:
                    continue
                start = first + par * 32 - (256 - width) - block * 256
                place = (tap % taps_x) * 32
                gsend[tap // taps_x, place:place + 32, :] = got[start:start + 32, :]
    step1 = []
    for t, (_, y_, n) in enumerate(order()):
        for d in range(1, nx):
            other = lax.rem(px + d, nx)
            m = t * (nx - 1) + d - 1
            part = piece(y_ * ring + n)
            step1.append(copy(gsend.at[other, part], g1.at[d - 1, t], s1s.at[m], s1r.at[m], x_peer(d)))
            step1[-1].start()

    gcols[:, 0:256] = grads
    for half in range(2):
        rows = slice(half * 256, half * 256 + 256)
        for n in range(1, 8):
            gcols[rows, n * 256:n * 256 + 256] = dot(shiftmt[n], grads[rows, :], NN).astype(BF16)
    for half in range(2):
        rows = slice(half * 256, half * 256 + 256)
        got = dot(gcols[rows, :], wcat[...], NT) * dsilu[rows, :]
        direct = dot(grads[rows, :], w27[...], NT)
        for n in range(4):
            one = got[n * 64:n * 64 + 64, :]
            slot = 4 * half + n
            send_i[slot, :, 0:128] = (one[:, 0:128] + direct[n * 64:n * 64 + 64, :]).astype(BF16)
            send_i[slot, :, 128:256] = one[:, 128:256].astype(BF16)
        got = dot(cols[rows, :], wf[...], NN)
        for n in range(4):
            send_o[4 * half + n] = got[n * 64:n * 64 + 64, :].astype(BF16)
    home = []
    for k in (3, 1, 2, 0):
        for e in (0, 1):
            if k == 0 and e == 0:
                continue
            s = e if k else 1 - core
            chip = (y, y - 1, y + 1, y - far(e))[k]
            slot = 2 * k + s
            dev = at(pz, chip, px, s)
            n = 2 * k + e
            home.append(copy(send_i.at[slot], recv_i.at[shard], is_.at[n], ir.at[shard], dev))
            home.append(copy(send_o.at[slot], recv_o.at[shard], os_.at[n], or_.at[shard], dev))
    pl.semaphore_wait(across, 1)
    step2 = []
    for t, (own, y_, n) in enumerate(order()):
        for d in range(1, nx):
            step1[t * (nx - 1) + d - 1].wait()
        part = y_ * ring + n
        total = gsend[px, piece(part), :].astype(F32)
        for d in range(1, nx):
            total = total + g1[d - 1, t].astype(F32)
        s2[part] = total.astype(BF16)
        send = copy(s2.at[part], r2.at[q], s2s.at[t], s2r.at[q], owner(y_, n))
        if not own:
            send.start()
            step2.append(send)
        elif ring < nz:
            pl.when(pz == IDLE)(send.start)
            last2 = send
    r2[q] = s2[mine]

    for send in home:
        send.start()
    recv_i[shard] = send_i[core]
    recv_o[shard] = send_o[core]

    def for_owners(body):
        if ring < nz:
            pl.when(is_owner)(body)
        else:
            body()

    part = piece(mine)
    step3 = [copy(fin.at[px, part], fin.at[px, part], s3s.at[t], s3r.at[q], owner(y_, n))
             for t, (own, y_, n) in enumerate(order()) if not own]
    if ring < nz:
        for n, y_ in enumerate((1 - y_hi, y_hi)):
            step3.append(copy(fin.at[px, part], fin.at[px, part], s3s.at[2 * ring + n], s3r.at[q],
                              at(IDLE, y_ * 4 + lax.rem(y, 4), px, core)))

    @for_owners
    def _():
        for d in range(1, nq):
            other = lax.rem(q + d, nq)
            copy(r2.at[other], r2.at[other], s2s.at[0], s2r.at[other], partner).wait_recv()
        fin[px, part, :] = jnp.sum(r2[...].astype(F32), axis=0).astype(BF16)
        for send in step3:
            send.start()

    step4 = []
    places = list(order())[::-1]
    for t, (own, y_, n) in enumerate(places):
        theirs = piece(y_ * ring + n)
        sender = y_ * nz + (n + lax.div(n, IDLE) if ring < nz else n)
        come = copy(fin.at[px, theirs], fin.at[px, theirs], s3s.at[0], s3r.at[sender], partner)
        if not own:
            come.wait_recv()
        elif ring < nz:
            pl.when(pz == IDLE)(come.wait_recv)
        for d in range(1, nx):
            m = t * (nx - 1) + d - 1
            step4.append(copy(fin.at[px, theirs], fin.at[px, theirs], s4s.at[m], s4r.at[m], x_peer(d)))
            step4[-1].start()

    for e in range(1, 8):
        slot = lax.rem(shard + e, 8)
        for buf, ssem, sem in ((recv_i, is_, ir), (recv_o, os_, or_)):
            copy(buf.at[slot], buf.at[slot], ssem.at[0], sem.at[slot], at(pz, y, px, 1 - core)).wait_recv()
    out_v[...] = jnp.sum(recv_o[...].astype(F32), axis=0).astype(BF16)
    for par in range(8):
        for h in range(2):
            sorted_x[par, :, h * 128:h * 128 + 128] = jnp.concatenate(
                [recv_i[4 * h + n, :, par * 32:par * 32 + 32].astype(F32) for n in range(4)], axis=1)
    for b in range(2):
        natural = sorted_x[:, b * 32:b * 32 + 32, :].reshape(256, 256).astype(BF16)
        ig_v[b * 256:b * 256 + 256, :] = dot(sortmt[...], natural, NN).astype(BF16)

    for t, (own, y_, n) in enumerate(places):
        theirs = piece(y_ * ring + n)
        for d in range(1, nx):
            m = t * (nx - 1) + d - 1
            other = lax.rem(px + nx - d, nx)
            copy(fin.at[other, theirs], fin.at[other, theirs], s4s.at[m], s4r.at[m], x_peer(d)).wait_recv()
    for send in sends + home + step2 + step4:
        send.wait_send()
    if ring < nz:
        pl.when(pz == IDLE)(last2.wait_send)

    @for_owners
    def _():
        for send in step3:
            send.wait_send()


def finish(out_v, ig_v, fin, out_hbm, ig_hbm, wg_hbm, out_s, wg_s, sem):
    nx, rows = wg_s.shape[:2]
    stores = [pltpu.make_async_copy(ig_v, ig_hbm, sem.at[0])]
    stores[0].start()
    for n in range(nx):
        wg_s[n] = fin[n, 0:rows, :].astype(F32)
        stores.append(pltpu.make_async_copy(wg_s.at[n], wg_hbm.at[n], sem.at[n + 1]))
        stores[-1].start()
    out_s[...] = out_v[...].astype(F32).reshape(4, 4, 4, 256).astype(BF16)
    stores.append(pltpu.make_async_copy(out_s, out_hbm, sem.at[nx + 1]))
    stores[-1].start()
    for store in stores:
        store.wait()


def shards(nx, nz, inputs, cotangent, weights):
    nq = 2 * nz
    owners = 14 if nz == 8 else nq
    rows_x = 28 // nx * 32
    rows_q = rows_x // owners
    dma = pltpu.SemaphoreType.DMA
    sems = [dma((n,)) for n in (3, 8, 8, 4, 8, 4, 8, 8, 8, 8)]
    sems += [dma((max(n, 1),)) for n in (owners * (nx - 1), owners * (nx - 1), nq, nq, nq, nq, owners * (nx - 1), owners * (nx - 1))]
    sems += [pltpu.SemaphoreType.REGULAR] * 3
    vm = pltpu.VMEM
    scratch = [
        vm((512, 256), BF16), vm((4, 4, 4, 256), BF16), vm((64, 256), BF16), vm((28, 32, 256), BF16),
        vm((256, 256), BF16), vm((256, 256), BF16), vm((8, 256, 256), BF16), vm((8, 256, 256), BF16),
        vm((8, 64, 256), F32), vm((8, 64, 256), BF16),
        vm((8, 64, 256), BF16), vm((8, 64, 256), BF16),
        vm((512, 1536), BF16), vm((512, 2048), BF16),
        vm((1536, 256), BF16), vm((256, 2048), BF16), vm((128, 256), BF16),
        vm((512, 256), F32),
        vm((8, 64, 256), BF16), vm((8, 64, 256), BF16),
        vm((8, 64, 256), BF16), vm((8, 64, 256), BF16),
        vm((nx, rows_x, 256), BF16), vm((max(nx - 1, 1), owners, rows_q, 256), BF16),
        vm((owners, rows_q, 256), BF16), vm((nq, rows_q, 256), BF16),
    ] + sems
    hbm = pl.BlockSpec(memory_space=pltpu.HBM)
    vmem = pl.BlockSpec(memory_space=pltpu.VMEM)
    out, ig, wg = pl.pallas_call(
        functools.partial(kernel, nx, nz),
        out_shape=(
            jax.ShapeDtypeStruct((64, 256), BF16),
            jax.ShapeDtypeStruct((512, 256), BF16),
            jax.ShapeDtypeStruct((nx, rows_x, 256), BF16),
        ),
        in_specs=[hbm] * 3,
        out_specs=(vmem,) * 3,
        scratch_shapes=scratch,
        compiler_params=pltpu.CompilerParams(
            collective_id=0, has_side_effects=True, vmem_limit_bytes=48 * 2**20),
        name="unit",
    )(*[pltpu.with_memory_space_constraint(a, pltpu.HBM)
        for a in (inputs.reshape(512, 256), cotangent.reshape(4, 4, 4, 256), weights)])
    out, ig, wg = pl.pallas_call(
        finish,
        out_shape=(
            jax.ShapeDtypeStruct((4, 4, 4, 256), BF16),
            jax.ShapeDtypeStruct((512, 256), BF16),
            jax.ShapeDtypeStruct((nx, rows_x, 256), F32),
        ),
        in_specs=[vmem] * 3,
        out_specs=(hbm,) * 3,
        scratch_shapes=[vm((4, 4, 4, 256), BF16), vm((nx, rows_x, 256), F32), dma((nx + 2,))],
        compiler_params=pltpu.CompilerParams(vmem_limit_bytes=8 * 2**20),
        name="finish",
    )(out, ig, wg)
    return (
        out.reshape(1, 4, 4, 4, 256),
        ig.reshape(1, 8, 8, 8, 256),
        wg.reshape(28, 32, 256),
    )


def solution(mesh, nx=4):
    nz = mesh.shape["dp"] // (2 * nx)
    rows = P(("dp", "shard"), None, None, None, None)
    return jax.shard_map(
        functools.partial(shards, nx, nz),
        mesh=mesh,
        in_specs=(rows, rows, P(None, "shard", None)),
        out_specs=(rows, rows, P(None, "shard", None)),
        check_vma=False,
    )
```

```python
import functools

import jax
import jax.numpy as jnp
from jax import lax
from jax.experimental import pallas as pl
from jax.experimental.pallas import tpu as pltpu
from jax.sharding import PartitionSpec as P

F32 = jnp.float32
BF16 = jnp.bfloat16
MESH = pl.DeviceIdType.MESH

COMBOS = [(si, sj, sk) for si in (0, -1) for sj in (0, -1) for sk in (0, -1)]
IDLE = 4
DIRECT = 2


def lane_of(combo):
    return (256 * combo, 256) if combo < 4 else (1024 + 128 * (combo - 4), 128)


def tap_of(combo, parity):
    total = 0
    for weight, shift, odd in zip((9, 3, 1), COMBOS[combo], parity):
        if shift and not odd:
            return None
        total += weight * (1 if not odd else 0 if shift else 2)
    return total


PARITIES = [(a, b, c) for a in (0, 1) for b in (0, 1) for c in (0, 1)]


def dot(a, b, dims):
    return lax.dot_general(a, b, (dims, ((), ())), preferred_element_type=F32)


NN = ((1,), (0,))
NT = ((1,), (1,))
TN = ((0,), (0,))


def one_hot(hit):
    return jnp.where(hit, 1.0, 0.0).astype(BF16)


def sort_target(rows):
    k, j, i = rows & 3, (rows >> 2) & 3, (rows >> 4) & 1
    pk, pj, pi = (rows >> 5) & 1, (rows >> 6) & 1, (rows >> 7) & 1
    return (2 * i + pi) * 64 + (2 * j + pj) * 8 + 2 * k + pk


def kernel(nx, nz, x_hbm, g_hbm, w_hbm, out_v, ig_v, fin,
           x_in, g_raw, g_in, w_in, sortm, sortmt, shiftm, shiftmt, sorted_x, send_x,
           recv_x, recv_g, cols, gcols, wf, wcat, w27, dsilu, send_o, recv_o,
           send_i, recv_i, gsend, g1, s2, r2,
           in_sem, xs, xr, gs, gr, fs, os_, or_, is_, ir, s1s, s1r, s2s, s2r,
           s3s, s3r, s4s, s4r, across):
    nq = 2 * nz
    taps_x = 28 // nx
    rows_q = s2.shape[1]
    ring = s2.shape[0]
    dp = lax.axis_index("dp")
    shard = lax.axis_index("shard")
    px = lax.rem(dp, nx)
    y_hi = lax.rem(lax.div(dp, nx), 2)
    pz = lax.div(dp, 2 * nx)
    y = y_hi * 4 + lax.div(shard, 2)
    core = lax.rem(shard, 2)
    sign = 1 - 2 * core
    q = y_hi * nz + pz

    def at(pz_, y_, px_, core_):
        y_ = lax.rem(y_ + 8, 8)
        return ((pz_ * 2 + lax.div(y_, 4)) * nx + px_, lax.rem(y_, 4) * 2 + core_)

    def slice_of(y_, core_):
        return lax.rem(y_ + 8, 4) * 2 + core_

    def x_peer(d):
        return at(pz, y, lax.rem(px + d, nx), core)

    def z_peer(d):
        return at(lax.rem(pz + d + nz, nz), y, px, core)

    here = lax.rem(pz - lax.div(pz, IDLE + 1), nz) if ring < nz else pz
    is_owner = (y_hi == 0) & (pz != IDLE) if ring < nz else y_hi == 0
    near_first = sorted(range(ring), key=lambda e: min(e, ring - e))
    order = [(e == 0, lax.rem(here + e, ring)) for e in near_first]

    def owner(n):
        return at(n + lax.div(n, IDLE) if ring < nz else n, lax.rem(y, 4), px, core)

    def piece(n):
        return pl.ds(pl.multiple_of(n * rows_q, 16), rows_q)

    partner = at(pz, y, px, 1 - core)

    def copy(src, dst, send, recv, dev):
        return pltpu.make_async_remote_copy(
            src_ref=src, dst_ref=dst, send_sem=send, recv_sem=recv, device_id=dev, device_id_type=MESH)

    def signal(sem, dev):
        pl.semaphore_signal(sem, inc=1, device_id=dev, device_id_type=MESH)

    loads = [pltpu.make_async_copy(a, b, in_sem.at[n]) for n, (a, b) in enumerate(((x_hbm, x_in), (g_hbm, g_raw), (w_hbm, w_in)))]
    for load in loads:
        load.start()

    peers = [partner]
    for d in (1, -1):
        for c in (0, 1):
            peers.append(at(pz, y + d, px, c))
    peers += [at(pz, y + 2 * sign, px, core), at(pz, y + 2 * sign, px, 1 - core), at(pz, y - 2 * sign, px, core)]
    peers += [x_peer(d) for d in range(1, nx)]
    peers += [z_peer(d) for d in range(1, nz)] + [at(pz, y + 4, px, core)]
    barrier = pltpu.get_barrier_semaphore()
    for peer in peers:
        signal(barrier, peer)

    row = lax.broadcasted_iota(jnp.int32, (256, 256), 0)
    col = lax.broadcasted_iota(jnp.int32, (256, 256), 1)
    sortm[...] = one_hot(sort_target(row) == col)
    loads[0].wait()
    for b in range(2):
        got = dot(sortm[...], x_in[b * 256:b * 256 + 256, :], NN)
        for par in range(8):
            sorted_x[par, b * 32:b * 32 + 32, :] = got[par * 32:par * 32 + 32, :]
    for p in range(8):
        for h in range(2):
            send_x[p, :, h * 128:h * 128 + 128] = jnp.concatenate(
                [sorted_x[4 * h + n, :, p * 32:p * 32 + 32] for n in range(4)], axis=1).astype(BF16)
    loads[1].wait()
    g_in[...] = g_raw[...].astype(F32).reshape(64, 256).astype(BF16)
    pl.semaphore_wait(barrier, len(peers))

    def far(c):
        return 2 - 4 * c

    def to_chip(k):
        return (y, y + 1, y - 1, y + 2 * sign)[k]

    sends = []
    for k in (3, 1, 2):
        slot = 2 * k + core
        sends.append(copy(g_in, recv_g.at[slot], gs.at[k], gr.at[slot], at(pz, to_chip(k), px, core)))
    sends.append(copy(g_in, recv_g.at[core], gs.at[0], gr.at[core], partner))
    for k in (3, 1, 2, 0):
        for e in (0, 1):
            if k == 0 and e == 0:
                continue
            c = lax.rem(core + e, 2)
            slot = 2 * k + core
            sends.append(copy(send_x.at[slice_of(to_chip(k), c)], recv_x.at[slot], xs.at[2 * k + e], xr.at[slot],
                              at(pz, to_chip(k), px, c)))
    signal(across, at(pz, y + 4, px, core))
    for send in sends:
        send.start()
    recv_x[core] = send_x[shard]
    recv_g[core] = g_in[...]

    sortmt[...] = one_hot(sort_target(col) == row)
    ri, rj, rk = (row >> 4) & 3, (row >> 2) & 3, row & 3
    ci, cj, ck = (col >> 4) & 3, (col >> 2) & 3, col & 3
    for n, (si, sj, sk) in enumerate(COMBOS):
        if n == 0:
            continue
        step = 16 * si + 4 * sj + sk
        ok = (col == row + step) & (ri >= -si) & (rj >= -sj) & (rk >= -sk)
        shiftm[n] = one_hot(ok)
        ok = (row == col + step) & (ci >= -si) & (cj >= -sj) & (ck >= -sk)
        shiftmt[n] = one_hot(ok)
    wf[...] = jnp.zeros_like(wf)
    wcat[...] = jnp.zeros_like(wcat)
    w27[...] = jnp.zeros_like(w27)
    loads[2].wait()
    for n in range(8):
        first, width = lane_of(n)
        for par, parity in enumerate(PARITIES):
            tap = tap_of(n, parity)
            if tap is None:
                continue
            at_row = first + par * 32 - (256 - width)
            wf[at_row:at_row + 32, :] = w_in[tap]
            wcat[par * 32:par * 32 + 32, n * 256:n * 256 + 256] = w_in[tap]
    first = lane_of(DIRECT)[0]
    wf[first:first + 32, :] = w_in[27]
    w27[0:32, :] = w_in[27]

    def arrived(buf, sem, slot):
        copy(buf.at[slot], buf.at[slot], xs.at[0], sem.at[slot], partner).wait_recv()

    for k in (1, 2, 3):
        slot = 2 * k + core
        arrived(recv_g, gr, slot)
        sends.append(copy(recv_g.at[slot], recv_g.at[slot], fs.at[k], gr.at[slot], partner))
        sends[-1].start()

    def returns(half):
        rows = slice(half * 256, half * 256 + 256)
        four = recv_g[4 * half:4 * half + 4].reshape(256, 256)
        gcols[rows, 0:256] = four
        for n in range(1, 8):
            gcols[rows, n * 256:n * 256 + 256] = dot(shiftmt[n], four, NN).astype(BF16)
        got = dot(gcols[rows, :], wcat[...], NT) * dsilu[rows, :]
        direct = dot(four, w27[...], NT)
        for n in range(4):
            one = got[n * 64:n * 64 + 64, :]
            slot = 4 * half + n
            send_i[slot, :, 0:128] = (one[:, 0:128] + direct[n * 64:n * 64 + 64, :]).astype(BF16)
            send_i[slot, :, 128:256] = one[:, 128:256].astype(BF16)
        got = dot(cols[rows, :], wf[...], NN)
        for n in range(4):
            send_o[4 * half + n] = got[n * 64:n * 64 + 64, :].astype(BF16)

    for half in range(2):
        rows = slice(half * 256, half * 256 + 256)
        for k in (2 * half, 2 * half + 1):
            for e in (0, 1):
                if k or e:
                    arrived(recv_x, xr, 2 * k + lax.rem(core + e, 2))
        raw = recv_x[4 * half:4 * half + 4].reshape(256, 256)
        v = raw.astype(F32)
        s = 1.0 / (1.0 + jnp.exp(-v))
        act = (v * s).astype(BF16)
        dsilu[rows, :] = s * (1.0 + v * (1.0 - s))
        cols[rows, 0:256] = act
        lane = lax.broadcasted_iota(jnp.int32, (256, 256), 1)
        for n in range(1, 8):
            first, width = lane_of(n)
            moved = dot(shiftm[n], act[:, 256 - width:], NN)
            if n == DIRECT:
                moved = jnp.where(lane < 32, v, moved)
            cols[rows, first:first + width] = moved.astype(BF16)
        for k in (2 * half, 2 * half + 1):
            arrived(recv_g, gr, 2 * k + 1 - core)
        if half == 0:
            returns(0)

    grads = recv_g[...].reshape(512, 256)
    for block in range(6):
        got = dot(cols[:, block * 256:block * 256 + 256], grads, TN).astype(BF16)
        for n in range(8):
            first, width = lane_of(n)
            if first // 256 != block:
                continue
            for par, parity in enumerate(PARITIES):
                tap = tap_of(n, parity)
                if n == DIRECT and par == 0:
                    tap = 27
                if tap is None:
                    continue
                start = first + par * 32 - (256 - width) - block * 256
                place = (tap % taps_x) * 32
                gsend[tap // taps_x, place:place + 32, :] = got[start:start + 32, :]
    step1 = []
    for t, (_, n) in enumerate(order[::-1]):
        for d in range(1, nx):
            other = lax.rem(px + d, nx)
            m = t * (nx - 1) + d - 1
            step1.append(copy(gsend.at[other, piece(n)], g1.at[d - 1, t], s1s.at[m], s1r.at[m], x_peer(d)))
            step1[-1].start()

    returns(1)
    home, home_o = [], []
    for k in (3, 1, 2, 0):
        for e in (0, 1):
            if k == 0 and e == 0:
                continue
            s = e if k else 1 - core
            chip = (y, y - 1, y + 1, y - far(e))[k]
            slot = 2 * k + s
            dev = at(pz, chip, px, s)
            n = 2 * k + e
            home.append(copy(send_i.at[slot], recv_i.at[shard], is_.at[n], ir.at[shard], dev))
            home_o.append(copy(send_o.at[slot], recv_o.at[shard], os_.at[n], or_.at[shard], dev))
    for send in home:
        send.start()
    recv_i[shard] = send_i[core]
    recv_o[shard] = send_o[core]

    pl.semaphore_wait(across, 1)
    step2 = []
    for t, (own, n) in enumerate(order[::-1]):
        for d in range(1, nx):
            step1[t * (nx - 1) + d - 1].wait()
        total = gsend[px, piece(n), :].astype(F32)
        for d in range(1, nx):
            total = total + g1[d - 1, t].astype(F32)
        s2[n] = total.astype(BF16)
        step2.append(copy(s2.at[n], r2.at[q], s2s.at[t], s2r.at[q], owner(n)))
        if own:
            pl.when(jnp.logical_not(is_owner))(step2[-1].start)
        else:
            step2[-1].start()
    r2[q] = s2[here]

    part = piece(here)
    step3 = []
    for y_ in (0, 1):
        for e in sorted(range(nz), key=lambda e: -min(e, nz - e)):
            if y_ or e:
                step3.append(copy(fin.at[px, part], fin.at[px, part], s3s.at[len(step3)], s3r.at[here],
                                  at(lax.rem(pz + e, nz), y_ * 4 + lax.rem(y, 4), px, core)))

    @pl.when(is_owner)
    def _():
        for d in range(1, nq):
            other = lax.rem(q + d, nq)
            copy(r2.at[other], r2.at[other], s2s.at[0], s2r.at[other], partner).wait_recv()
        fin[px, part, :] = jnp.sum(r2[...].astype(F32), axis=0).astype(BF16)
        for send in step3:
            send.start()

    for send in home_o:
        send.start()
    step4 = []
    for t, (own, n) in enumerate(order):
        come = copy(fin.at[px, piece(n)], fin.at[px, piece(n)], s3s.at[0], s3r.at[n], partner)
        if own:
            pl.when(jnp.logical_not(is_owner))(come.wait_recv)
        else:
            come.wait_recv()
        for d in range(1, nx):
            m = t * (nx - 1) + d - 1
            step4.append(copy(fin.at[px, piece(n)], fin.at[px, piece(n)], s4s.at[m], s4r.at[m], x_peer(d)))
            step4[-1].start()

    for e in range(1, 8):
        slot = lax.rem(shard + e, 8)
        for buf, ssem, sem in ((recv_i, is_, ir), (recv_o, os_, or_)):
            copy(buf.at[slot], buf.at[slot], ssem.at[0], sem.at[slot], at(pz, y, px, 1 - core)).wait_recv()
    out_v[...] = jnp.sum(recv_o[...].astype(F32), axis=0).astype(BF16)
    for par in range(8):
        for h in range(2):
            sorted_x[par, :, h * 128:h * 128 + 128] = jnp.concatenate(
                [recv_i[4 * h + n, :, par * 32:par * 32 + 32].astype(F32) for n in range(4)], axis=1)
    for b in range(2):
        natural = sorted_x[:, b * 32:b * 32 + 32, :].reshape(256, 256).astype(BF16)
        ig_v[b * 256:b * 256 + 256, :] = dot(sortmt[...], natural, NN).astype(BF16)

    for t, (_, n) in enumerate(order):
        for d in range(1, nx):
            m = t * (nx - 1) + d - 1
            other = lax.rem(px + nx - d, nx)
            copy(fin.at[other, piece(n)], fin.at[other, piece(n)], s4s.at[m], s4r.at[m], x_peer(d)).wait_recv()
    for send in sends + home + home_o + step2[:-1] + step4:
        send.wait_send()
    pl.when(jnp.logical_not(is_owner))(step2[-1].wait_send)

    @pl.when(is_owner)
    def _():
        for send in step3:
            send.wait_send()


def finish(out_v, ig_v, fin, out_hbm, ig_hbm, wg_hbm, out_s, wg_s, sem):
    nx, rows = wg_s.shape[:2]
    stores = [pltpu.make_async_copy(ig_v, ig_hbm, sem.at[0])]
    stores[0].start()
    for n in range(nx):
        wg_s[n] = fin[n, 0:rows, :].astype(F32)
        stores.append(pltpu.make_async_copy(wg_s.at[n], wg_hbm.at[n], sem.at[n + 1]))
        stores[-1].start()
    out_s[...] = out_v[...].astype(F32).reshape(4, 4, 4, 256).astype(BF16)
    stores.append(pltpu.make_async_copy(out_s, out_hbm, sem.at[nx + 1]))
    stores[-1].start()
    for store in stores:
        store.wait()


def shards(nx, nz, inputs, cotangent, weights):
    nq = 2 * nz
    owners = 7 if nz == 8 else nz
    rows_x = 28 // nx * 32
    rows_q = rows_x // owners
    dma = pltpu.SemaphoreType.DMA
    sems = [dma((n,)) for n in (3, 8, 8, 4, 8, 4, 8, 8, 8, 8)]
    sems += [dma((max(n, 1),)) for n in (owners * (nx - 1), owners * (nx - 1), nq, nq, nq, nq, owners * (nx - 1), owners * (nx - 1))]
    sems += [pltpu.SemaphoreType.REGULAR]
    vm = pltpu.VMEM
    scratch = [
        vm((512, 256), BF16), vm((4, 4, 4, 256), BF16), vm((64, 256), BF16), vm((28, 32, 256), BF16),
        vm((256, 256), BF16), vm((256, 256), BF16), vm((8, 256, 256), BF16), vm((8, 256, 256), BF16),
        vm((8, 64, 256), F32), vm((8, 64, 256), BF16),
        vm((8, 64, 256), BF16), vm((8, 64, 256), BF16),
        vm((512, 1536), BF16), vm((512, 2048), BF16),
        vm((1536, 256), BF16), vm((256, 2048), BF16), vm((128, 256), BF16),
        vm((512, 256), F32),
        vm((8, 64, 256), BF16), vm((8, 64, 256), BF16),
        vm((8, 64, 256), BF16), vm((8, 64, 256), BF16),
        vm((nx, rows_x, 256), BF16), vm((max(nx - 1, 1), owners, rows_q, 256), BF16),
        vm((owners, rows_q, 256), BF16), vm((nq, rows_q, 256), BF16),
    ] + sems
    hbm = pl.BlockSpec(memory_space=pltpu.HBM)
    vmem = pl.BlockSpec(memory_space=pltpu.VMEM)
    out, ig, wg = pl.pallas_call(
        functools.partial(kernel, nx, nz),
        out_shape=(
            jax.ShapeDtypeStruct((64, 256), BF16),
            jax.ShapeDtypeStruct((512, 256), BF16),
            jax.ShapeDtypeStruct((nx, rows_x, 256), BF16),
        ),
        in_specs=[hbm] * 3,
        out_specs=(vmem,) * 3,
        scratch_shapes=scratch,
        compiler_params=pltpu.CompilerParams(
            collective_id=0, has_side_effects=True, vmem_limit_bytes=48 * 2**20),
        name="unit",
    )(*[pltpu.with_memory_space_constraint(a, pltpu.HBM)
        for a in (inputs.reshape(512, 256), cotangent.reshape(4, 4, 4, 256), weights)])
    out, ig, wg = pl.pallas_call(
        finish,
        out_shape=(
            jax.ShapeDtypeStruct((4, 4, 4, 256), BF16),
            jax.ShapeDtypeStruct((512, 256), BF16),
            jax.ShapeDtypeStruct((nx, rows_x, 256), F32),
        ),
        in_specs=[vmem] * 3,
        out_specs=(hbm,) * 3,
        scratch_shapes=[vm((4, 4, 4, 256), BF16), vm((nx, rows_x, 256), F32), dma((nx + 2,))],
        compiler_params=pltpu.CompilerParams(vmem_limit_bytes=8 * 2**20),
        name="finish",
    )(out, ig, wg)
    return (
        out.reshape(1, 4, 4, 4, 256),
        ig.reshape(1, 8, 8, 8, 256),
        wg.reshape(28, 32, 256),
    )


def solution(mesh, nx=4):
    nz = mesh.shape["dp"] // (2 * nx)
    rows = P(("dp", "shard"), None, None, None, None)
    return jax.shard_map(
        functools.partial(shards, nx, nz),
        mesh=mesh,
        in_specs=(rows, rows, P(None, "shard", None)),
        out_specs=(rows, rows, P(None, "shard", None)),
        check_vma=False,
    )
```

```python
import functools

import jax
import jax.numpy as jnp
from jax import lax
from jax.experimental import pallas as pl
from jax.experimental.pallas import tpu as pltpu
from jax.sharding import PartitionSpec as P

F32 = jnp.float32
BF16 = jnp.bfloat16
MESH = pl.DeviceIdType.MESH

COMBOS = [(si, sj, sk) for si in (0, -1) for sj in (0, -1) for sk in (0, -1)]
IDLE = 4
DIRECT = 2


def lane_of(combo):
    return (256 * combo, 256) if combo < 4 else (1024 + 128 * (combo - 4), 128)


def tap_of(combo, parity):
    total = 0
    for weight, shift, odd in zip((9, 3, 1), COMBOS[combo], parity):
        if shift and not odd:
            return None
        total += weight * (1 if not odd else 0 if shift else 2)
    return total


PARITIES = [(a, b, c) for a in (0, 1) for b in (0, 1) for c in (0, 1)]


def dot(a, b, dims):
    return lax.dot_general(a, b, (dims, ((), ())), preferred_element_type=F32)


NN = ((1,), (0,))
NT = ((1,), (1,))
TN = ((0,), (0,))


def one_hot(hit):
    return jnp.where(hit, 1.0, 0.0).astype(BF16)


def sort_target(rows):
    k, j, i = rows & 3, (rows >> 2) & 3, (rows >> 4) & 1
    pk, pj, pi = (rows >> 5) & 1, (rows >> 6) & 1, (rows >> 7) & 1
    return (2 * i + pi) * 64 + (2 * j + pj) * 8 + 2 * k + pk


def kernel(nx, nz, x_hbm, g_hbm, w_hbm, out_v, ig_v, fin,
           x_in, g_raw, g_in, w_in, sortm, sortmt, shiftm, shiftmt, sorted_x, send_x,
           recv_x, recv_g, cols, gcols, wf, wcat, w27, dsilu, send_o, recv_o,
           send_i, recv_i, gsend, g1, s2, r2,
           in_sem, xs, xr, gs, gr, fs, os_, or_, is_, ir, s1s, s1r, s2s, s2r,
           s3s, s3r, s4s, s4r, across):
    nq = 2 * nz
    taps_x = 28 // nx
    rows_q = s2.shape[1]
    ring = s2.shape[0] // 2
    dp = lax.axis_index("dp")
    shard = lax.axis_index("shard")
    px = lax.rem(dp, nx)
    y_hi = lax.rem(lax.div(dp, nx), 2)
    pz = lax.div(dp, 2 * nx)
    y = y_hi * 4 + lax.div(shard, 2)
    core = lax.rem(shard, 2)
    sign = 1 - 2 * core
    q = y_hi * nz + pz

    def at(pz_, y_, px_, core_):
        y_ = lax.rem(y_ + 8, 8)
        return ((pz_ * 2 + lax.div(y_, 4)) * nx + px_, lax.rem(y_, 4) * 2 + core_)

    def slice_of(y_, core_):
        return lax.rem(y_ + 8, 4) * 2 + core_

    def x_peer(d):
        return at(pz, y, lax.rem(px + d, nx), core)

    def z_peer(d):
        return at(lax.rem(pz + d + nz, nz), y, px, core)

    here = lax.rem(pz - lax.div(pz, IDLE + 1), nz) if ring < nz else pz
    is_owner = pz != IDLE
    mine = y_hi * ring + here

    def owner(y_, n):
        return at(n + lax.div(n, IDLE) if ring < nz else n, y_ * 4 + lax.rem(y, 4), px, core)

    def order():
        offsets = sorted(range(ring), key=lambda e: -min(e, ring - e))
        for other_y in (1, 0):
            for e in offsets:
                y_ = 1 - y_hi if other_y else y_hi
                yield not other_y and e == 0, y_, lax.rem(here + e, ring)

    def piece(n):
        return pl.ds(pl.multiple_of(n * rows_q, 16), rows_q)

    partner = at(pz, y, px, 1 - core)

    def copy(src, dst, send, recv, dev):
        return pltpu.make_async_remote_copy(
            src_ref=src, dst_ref=dst, send_sem=send, recv_sem=recv, device_id=dev, device_id_type=MESH)

    def signal(sem, dev):
        pl.semaphore_signal(sem, inc=1, device_id=dev, device_id_type=MESH)

    loads = [pltpu.make_async_copy(a, b, in_sem.at[n]) for n, (a, b) in enumerate(((x_hbm, x_in), (g_hbm, g_raw), (w_hbm, w_in)))]
    for load in loads:
        load.start()

    peers = [partner]
    for d in (1, -1):
        for c in (0, 1):
            peers.append(at(pz, y + d, px, c))
    peers += [at(pz, y + 2 * sign, px, core), at(pz, y + 2 * sign, px, 1 - core), at(pz, y - 2 * sign, px, core)]
    peers += [x_peer(d) for d in range(1, nx)]
    peers += [z_peer(d) for d in range(1, nz)] + [at(pz, y + 4, px, core)]
    barrier = pltpu.get_barrier_semaphore()
    for peer in peers:
        signal(barrier, peer)

    row = lax.broadcasted_iota(jnp.int32, (256, 256), 0)
    col = lax.broadcasted_iota(jnp.int32, (256, 256), 1)
    sortm[...] = one_hot(sort_target(row) == col)
    loads[0].wait()
    for b in range(2):
        got = dot(sortm[...], x_in[b * 256:b * 256 + 256, :], NN)
        for par in range(8):
            sorted_x[par, b * 32:b * 32 + 32, :] = got[par * 32:par * 32 + 32, :]
    for p in range(8):
        for h in range(2):
            send_x[p, :, h * 128:h * 128 + 128] = jnp.concatenate(
                [sorted_x[4 * h + n, :, p * 32:p * 32 + 32] for n in range(4)], axis=1).astype(BF16)
    loads[1].wait()
    g_in[...] = g_raw[...].astype(F32).reshape(64, 256).astype(BF16)
    pl.semaphore_wait(barrier, len(peers))

    def far(c):
        return 2 - 4 * c

    def to_chip(k):
        return (y, y + 1, y - 1, y + 2 * sign)[k]

    sends = []
    for k in (3, 1, 2):
        slot = 2 * k + core
        sends.append(copy(g_in, recv_g.at[slot], gs.at[k], gr.at[slot], at(pz, to_chip(k), px, core)))
    sends.append(copy(g_in, recv_g.at[core], gs.at[0], gr.at[core], partner))
    for k in (3, 1, 2, 0):
        for e in (0, 1):
            if k == 0 and e == 0:
                continue
            c = lax.rem(core + e, 2)
            slot = 2 * k + core
            sends.append(copy(send_x.at[slice_of(to_chip(k), c)], recv_x.at[slot], xs.at[2 * k + e], xr.at[slot],
                              at(pz, to_chip(k), px, c)))
    signal(across, at(pz, y + 4, px, core))
    for send in sends:
        send.start()
    recv_x[core] = send_x[shard]
    recv_g[core] = g_in[...]

    sortmt[...] = one_hot(sort_target(col) == row)
    ri, rj, rk = (row >> 4) & 3, (row >> 2) & 3, row & 3
    ci, cj, ck = (col >> 4) & 3, (col >> 2) & 3, col & 3
    for n, (si, sj, sk) in enumerate(COMBOS):
        if n == 0:
            continue
        step = 16 * si + 4 * sj + sk
        ok = (col == row + step) & (ri >= -si) & (rj >= -sj) & (rk >= -sk)
        shiftm[n] = one_hot(ok)
        ok = (row == col + step) & (ci >= -si) & (cj >= -sj) & (ck >= -sk)
        shiftmt[n] = one_hot(ok)
    wf[...] = jnp.zeros_like(wf)
    wcat[...] = jnp.zeros_like(wcat)
    w27[...] = jnp.zeros_like(w27)
    loads[2].wait()
    for n in range(8):
        first, width = lane_of(n)
        for par, parity in enumerate(PARITIES):
            tap = tap_of(n, parity)
            if tap is None:
                continue
            at_row = first + par * 32 - (256 - width)
            wf[at_row:at_row + 32, :] = w_in[tap]
            wcat[par * 32:par * 32 + 32, n * 256:n * 256 + 256] = w_in[tap]
    first = lane_of(DIRECT)[0]
    wf[first:first + 32, :] = w_in[27]
    w27[0:32, :] = w_in[27]

    def arrived(buf, sem, slot):
        copy(buf.at[slot], buf.at[slot], xs.at[0], sem.at[slot], partner).wait_recv()

    for k in (1, 2, 3):
        slot = 2 * k + core
        arrived(recv_g, gr, slot)
        sends.append(copy(recv_g.at[slot], recv_g.at[slot], fs.at[k], gr.at[slot], partner))
        sends[-1].start()

    for half in range(2):
        rows = slice(half * 256, half * 256 + 256)
        for k in (2 * half, 2 * half + 1):
            for e in (0, 1):
                if k or e:
                    arrived(recv_x, xr, 2 * k + lax.rem(core + e, 2))
        raw = recv_x[4 * half:4 * half + 4].reshape(256, 256)
        v = raw.astype(F32)
        s = 1.0 / (1.0 + jnp.exp(-v))
        act = (v * s).astype(BF16)
        dsilu[rows, :] = s * (1.0 + v * (1.0 - s))
        cols[rows, 0:256] = act
        lane = lax.broadcasted_iota(jnp.int32, (256, 256), 1)
        for n in range(1, 8):
            first, width = lane_of(n)
            moved = dot(shiftm[n], act[:, 256 - width:], NN)
            if n == DIRECT:
                moved = jnp.where(lane < 32, v, moved)
            cols[rows, first:first + width] = moved.astype(BF16)

    for k in range(4):
        arrived(recv_g, gr, 2 * k + 1 - core)

    grads = recv_g[...].reshape(512, 256)
    for block in range(6):
        got = dot(cols[:, block * 256:block * 256 + 256], grads, TN).astype(BF16)
        for n in range(8):
            first, width = lane_of(n)
            if first // 256 != block:
                continue
            for par, parity in enumerate(PARITIES):
                tap = tap_of(n, parity)
                if n == DIRECT and par == 0:
                    tap = 27
                if tap is None:
                    continue
                start = first + par * 32 - (256 - width) - block * 256
                place = (tap % taps_x) * 32
                gsend[tap // taps_x, place:place + 32, :] = got[start:start + 32, :]
    step1 = []
    for t, (_, y_, n) in enumerate(order()):
        for d in range(1, nx):
            other = lax.rem(px + d, nx)
            m = t * (nx - 1) + d - 1
            part = piece(y_ * ring + n)
            step1.append(copy(gsend.at[other, part], g1.at[d - 1, t], s1s.at[m], s1r.at[m], x_peer(d)))
            step1[-1].start()

    gcols[:, 0:256] = grads
    for half in range(2):
        rows = slice(half * 256, half * 256 + 256)
        for n in range(1, 8):
            gcols[rows, n * 256:n * 256 + 256] = dot(shiftmt[n], grads[rows, :], NN).astype(BF16)
    for half in range(2):
        rows = slice(half * 256, half * 256 + 256)
        got = dot(gcols[rows, :], wcat[...], NT) * dsilu[rows, :]
        direct = dot(grads[rows, :], w27[...], NT)
        for n in range(4):
            one = got[n * 64:n * 64 + 64, :]
            slot = 4 * half + n
            send_i[slot, :, 0:128] = (one[:, 0:128] + direct[n * 64:n * 64 + 64, :]).astype(BF16)
            send_i[slot, :, 128:256] = one[:, 128:256].astype(BF16)
        got = dot(cols[rows, :], wf[...], NN)
        for n in range(4):
            send_o[4 * half + n] = got[n * 64:n * 64 + 64, :].astype(BF16)
    home = []
    for k in (3, 1, 2, 0):
        for e in (0, 1):
            if k == 0 and e == 0:
                continue
            s = e if k else 1 - core
            chip = (y, y - 1, y + 1, y - far(e))[k]
            slot = 2 * k + s
            dev = at(pz, chip, px, s)
            n = 2 * k + e
            home.append(copy(send_i.at[slot], recv_i.at[shard], is_.at[n], ir.at[shard], dev))
            home.append(copy(send_o.at[slot], recv_o.at[shard], os_.at[n], or_.at[shard], dev))
    pl.semaphore_wait(across, 1)
    step2 = []
    for t, (own, y_, n) in enumerate(order()):
        for d in range(1, nx):
            step1[t * (nx - 1) + d - 1].wait()
        part = y_ * ring + n
        total = gsend[px, piece(part), :].astype(F32)
        for d in range(1, nx):
            total = total + g1[d - 1, t].astype(F32)
        s2[part] = total.astype(BF16)
        send = copy(s2.at[part], r2.at[q], s2s.at[t], s2r.at[q], owner(y_, n))
        if not own:
            send.start()
            step2.append(send)
        elif ring < nz:
            pl.when(pz == IDLE)(send.start)
            last2 = send
    r2[q] = s2[mine]

    recv_i[shard] = send_i[core]
    recv_o[shard] = send_o[core]

    def for_owners(body):
        if ring < nz:
            pl.when(is_owner)(body)
        else:
            body()

    part = piece(mine)
    step3 = [copy(fin.at[px, part], fin.at[px, part], s3s.at[t], s3r.at[q], owner(y_, n))
             for t, (own, y_, n) in enumerate(order()) if not own]
    if ring < nz:
        for n, y_ in enumerate((1 - y_hi, y_hi)):
            step3.append(copy(fin.at[px, part], fin.at[px, part], s3s.at[2 * ring + n], s3r.at[q],
                              at(IDLE, y_ * 4 + lax.rem(y, 4), px, core)))

    @for_owners
    def _():
        for d in range(1, nq):
            other = lax.rem(q + d, nq)
            copy(r2.at[other], r2.at[other], s2s.at[0], s2r.at[other], partner).wait_recv()
        fin[px, part, :] = jnp.sum(r2[...].astype(F32), axis=0).astype(BF16)
        for send in step3:
            send.start()

    for send in home:
        send.start()
    step4 = []
    places = list(order())[::-1]
    for t, (own, y_, n) in enumerate(places):
        theirs = piece(y_ * ring + n)
        sender = y_ * nz + (n + lax.div(n, IDLE) if ring < nz else n)
        come = copy(fin.at[px, theirs], fin.at[px, theirs], s3s.at[0], s3r.at[sender], partner)
        if not own:
            come.wait_recv()
        elif ring < nz:
            pl.when(pz == IDLE)(come.wait_recv)
        for d in range(1, nx):
            m = t * (nx - 1) + d - 1
            step4.append(copy(fin.at[px, theirs], fin.at[px, theirs], s4s.at[m], s4r.at[m], x_peer(d)))
            step4[-1].start()

    for e in range(1, 8):
        slot = lax.rem(shard + e, 8)
        for buf, ssem, sem in ((recv_i, is_, ir), (recv_o, os_, or_)):
            copy(buf.at[slot], buf.at[slot], ssem.at[0], sem.at[slot], at(pz, y, px, 1 - core)).wait_recv()
    out_v[...] = jnp.sum(recv_o[...].astype(F32), axis=0).astype(BF16)
    for par in range(8):
        for h in range(2):
            sorted_x[par, :, h * 128:h * 128 + 128] = jnp.concatenate(
                [recv_i[4 * h + n, :, par * 32:par * 32 + 32].astype(F32) for n in range(4)], axis=1)
    for b in range(2):
        natural = sorted_x[:, b * 32:b * 32 + 32, :].reshape(256, 256).astype(BF16)
        ig_v[b * 256:b * 256 + 256, :] = dot(sortmt[...], natural, NN).astype(BF16)

    for t, (own, y_, n) in enumerate(places):
        theirs = piece(y_ * ring + n)
        for d in range(1, nx):
            m = t * (nx - 1) + d - 1
            other = lax.rem(px + nx - d, nx)
            copy(fin.at[other, theirs], fin.at[other, theirs], s4s.at[m], s4r.at[m], x_peer(d)).wait_recv()
    for send in sends + home + step2 + step4:
        send.wait_send()
    if ring < nz:
        pl.when(pz == IDLE)(last2.wait_send)

    @for_owners
    def _():
        for send in step3:
            send.wait_send()


def finish(out_v, ig_v, fin, out_hbm, ig_hbm, wg_hbm, out_s, wg_s, sem):
    nx, rows = wg_s.shape[:2]
    stores = [pltpu.make_async_copy(ig_v, ig_hbm, sem.at[0])]
    stores[0].start()
    for n in range(nx):
        wg_s[n] = fin[n, 0:rows, :].astype(F32)
        stores.append(pltpu.make_async_copy(wg_s.at[n], wg_hbm.at[n], sem.at[n + 1]))
        stores[-1].start()
    out_s[...] = out_v[...].astype(F32).reshape(4, 4, 4, 256).astype(BF16)
    stores.append(pltpu.make_async_copy(out_s, out_hbm, sem.at[nx + 1]))
    stores[-1].start()
    for store in stores:
        store.wait()


def shards(nx, nz, inputs, cotangent, weights):
    nq = 2 * nz
    owners = 14 if nz == 8 else nq
    rows_x = 28 // nx * 32
    rows_q = rows_x // owners
    dma = pltpu.SemaphoreType.DMA
    sems = [dma((n,)) for n in (3, 8, 8, 4, 8, 4, 8, 8, 8, 8)]
    sems += [dma((max(n, 1),)) for n in (owners * (nx - 1), owners * (nx - 1), nq, nq, nq, nq, owners * (nx - 1), owners * (nx - 1))]
    sems += [pltpu.SemaphoreType.REGULAR]
    vm = pltpu.VMEM
    scratch = [
        vm((512, 256), BF16), vm((4, 4, 4, 256), BF16), vm((64, 256), BF16), vm((28, 32, 256), BF16),
        vm((256, 256), BF16), vm((256, 256), BF16), vm((8, 256, 256), BF16), vm((8, 256, 256), BF16),
        vm((8, 64, 256), F32), vm((8, 64, 256), BF16),
        vm((8, 64, 256), BF16), vm((8, 64, 256), BF16),
        vm((512, 1536), BF16), vm((512, 2048), BF16),
        vm((1536, 256), BF16), vm((256, 2048), BF16), vm((128, 256), BF16),
        vm((512, 256), F32),
        vm((8, 64, 256), BF16), vm((8, 64, 256), BF16),
        vm((8, 64, 256), BF16), vm((8, 64, 256), BF16),
        vm((nx, rows_x, 256), BF16), vm((max(nx - 1, 1), owners, rows_q, 256), BF16),
        vm((owners, rows_q, 256), BF16), vm((nq, rows_q, 256), BF16),
    ] + sems
    hbm = pl.BlockSpec(memory_space=pltpu.HBM)
    vmem = pl.BlockSpec(memory_space=pltpu.VMEM)
    out, ig, wg = pl.pallas_call(
        functools.partial(kernel, nx, nz),
        out_shape=(
            jax.ShapeDtypeStruct((64, 256), BF16),
            jax.ShapeDtypeStruct((512, 256), BF16),
            jax.ShapeDtypeStruct((nx, rows_x, 256), BF16),
        ),
        in_specs=[hbm] * 3,
        out_specs=(vmem,) * 3,
        scratch_shapes=scratch,
        compiler_params=pltpu.CompilerParams(
            collective_id=0, has_side_effects=True, vmem_limit_bytes=48 * 2**20),
        name="unit",
    )(*[pltpu.with_memory_space_constraint(a, pltpu.HBM)
        for a in (inputs.reshape(512, 256), cotangent.reshape(4, 4, 4, 256), weights)])
    out, ig, wg = pl.pallas_call(
        finish,
        out_shape=(
            jax.ShapeDtypeStruct((4, 4, 4, 256), BF16),
            jax.ShapeDtypeStruct((512, 256), BF16),
            jax.ShapeDtypeStruct((nx, rows_x, 256), F32),
        ),
        in_specs=[vmem] * 3,
        out_specs=(hbm,) * 3,
        scratch_shapes=[vm((4, 4, 4, 256), BF16), vm((nx, rows_x, 256), F32), dma((nx + 2,))],
        compiler_params=pltpu.CompilerParams(vmem_limit_bytes=8 * 2**20),
        name="finish",
    )(out, ig, wg)
    return (
        out.reshape(1, 4, 4, 4, 256),
        ig.reshape(1, 8, 8, 8, 256),
        wg.reshape(28, 32, 256),
    )


def solution(mesh, nx=4):
    nz = mesh.shape["dp"] // (2 * nx)
    rows = P(("dp", "shard"), None, None, None, None)
    return jax.shard_map(
        functools.partial(shards, nx, nz),
        mesh=mesh,
        in_specs=(rows, rows, P(None, "shard", None)),
        out_specs=(rows, rows, P(None, "shard", None)),
        check_vma=False,
    )
```

```python
import functools

import jax
import jax.numpy as jnp
from jax import lax
from jax.experimental import pallas as pl
from jax.experimental.pallas import tpu as pltpu
from jax.sharding import PartitionSpec as P

F32 = jnp.float32
BF16 = jnp.bfloat16
MESH = pl.DeviceIdType.MESH

COMBOS = [(si, sj, sk) for si in (0, -1) for sj in (0, -1) for sk in (0, -1)]
IDLE = 4
DIRECT = 2


def lane_of(combo):
    return (256 * combo, 256) if combo < 4 else (1024 + 128 * (combo - 4), 128)


def tap_of(combo, parity):
    total = 0
    for weight, shift, odd in zip((9, 3, 1), COMBOS[combo], parity):
        if shift and not odd:
            return None
        total += weight * (1 if not odd else 0 if shift else 2)
    return total


PARITIES = [(a, b, c) for a in (0, 1) for b in (0, 1) for c in (0, 1)]


def dot(a, b, dims):
    return lax.dot_general(a, b, (dims, ((), ())), preferred_element_type=F32)


NN = ((1,), (0,))
NT = ((1,), (1,))
TN = ((0,), (0,))


def one_hot(hit):
    return jnp.where(hit, 1.0, 0.0).astype(BF16)


def sort_target(rows):
    k, j, i = rows & 3, (rows >> 2) & 3, (rows >> 4) & 1
    pk, pj, pi = (rows >> 5) & 1, (rows >> 6) & 1, (rows >> 7) & 1
    return (2 * i + pi) * 64 + (2 * j + pj) * 8 + 2 * k + pk


def kernel(nx, nz, x_hbm, g_hbm, w_hbm, out_v, ig_v, fin,
           x_in, g_raw, g_in, w_in, sortm, sortmt, shiftm, shiftmt, sorted_x, send_x,
           recv_x, recv_g, cols, gcols, wf, wcat, w27, dsilu, acc, send_o, recv_o,
           send_i, recv_i, gsend, g1, s2, r2,
           in_sem, xs, xr, gs, gr, fs, os_, or_, is_, ir, s1s, s1r, s2s, s2r,
           s3s, s3r, s4s, s4r, across):
    nq = 2 * nz
    taps_x = 28 // nx
    rows_q = s2.shape[1]
    ring = s2.shape[0] // 2
    dp = lax.axis_index("dp")
    shard = lax.axis_index("shard")
    px = lax.rem(dp, nx)
    y_hi = lax.rem(lax.div(dp, nx), 2)
    pz = lax.div(dp, 2 * nx)
    y = y_hi * 4 + lax.div(shard, 2)
    core = lax.rem(shard, 2)
    sign = 1 - 2 * core
    q = y_hi * nz + pz

    def at(pz_, y_, px_, core_):
        y_ = lax.rem(y_ + 8, 8)
        return ((pz_ * 2 + lax.div(y_, 4)) * nx + px_, lax.rem(y_, 4) * 2 + core_)

    def slice_of(y_, core_):
        return lax.rem(y_ + 8, 4) * 2 + core_

    def x_peer(d):
        return at(pz, y, lax.rem(px + d, nx), core)

    def z_peer(d):
        return at(lax.rem(pz + d + nz, nz), y, px, core)

    here = lax.rem(pz - lax.div(pz, IDLE + 1), nz) if ring < nz else pz
    is_owner = pz != IDLE
    mine = y_hi * ring + here

    def owner(y_, n):
        return at(n + lax.div(n, IDLE) if ring < nz else n, y_ * 4 + lax.rem(y, 4), px, core)

    def order():
        offsets = sorted(range(ring), key=lambda e: -min(e, ring - e))
        for other_y in (1, 0):
            for e in offsets:
                y_ = 1 - y_hi if other_y else y_hi
                yield not other_y and e == 0, y_, lax.rem(here + e, ring)

    def piece(n):
        return pl.ds(pl.multiple_of(n * rows_q, 16), rows_q)

    partner = at(pz, y, px, 1 - core)

    def copy(src, dst, send, recv, dev):
        return pltpu.make_async_remote_copy(
            src_ref=src, dst_ref=dst, send_sem=send, recv_sem=recv, device_id=dev, device_id_type=MESH)

    def signal(sem, dev):
        pl.semaphore_signal(sem, inc=1, device_id=dev, device_id_type=MESH)

    loads = [pltpu.make_async_copy(a, b, in_sem.at[n]) for n, (a, b) in enumerate(((x_hbm, x_in), (g_hbm, g_raw), (w_hbm, w_in)))]
    for load in loads:
        load.start()

    peers = [partner]
    for d in (1, -1):
        for c in (0, 1):
            peers.append(at(pz, y + d, px, c))
    peers += [at(pz, y + 2 * sign, px, core), at(pz, y + 2 * sign, px, 1 - core), at(pz, y - 2 * sign, px, core)]
    peers += [x_peer(d) for d in range(1, nx)]
    peers += [z_peer(d) for d in range(1, nz)] + [at(pz, y + 4, px, core)]
    barrier = pltpu.get_barrier_semaphore()
    for peer in peers:
        signal(barrier, peer)

    row = lax.broadcasted_iota(jnp.int32, (256, 256), 0)
    col = lax.broadcasted_iota(jnp.int32, (256, 256), 1)
    sortm[...] = one_hot(sort_target(row) == col)
    loads[0].wait()
    for b in range(2):
        got = dot(sortm[...], x_in[b * 256:b * 256 + 256, :], NN)
        for par in range(8):
            sorted_x[par, b * 32:b * 32 + 32, :] = got[par * 32:par * 32 + 32, :]
    for p in range(8):
        for h in range(2):
            send_x[p, :, h * 128:h * 128 + 128] = jnp.concatenate(
                [sorted_x[4 * h + n, :, p * 32:p * 32 + 32] for n in range(4)], axis=1).astype(BF16)
    loads[1].wait()
    g_in[...] = g_raw[...].astype(F32).reshape(64, 256).astype(BF16)
    pl.semaphore_wait(barrier, len(peers))

    def far(c):
        return 2 - 4 * c

    def to_chip(k):
        return (y, y + 1, y - 1, y + 2 * sign)[k]

    sends = []
    for k in (3, 1, 2):
        slot = 2 * k + core
        sends.append(copy(g_in, recv_g.at[slot], gs.at[k], gr.at[slot], at(pz, to_chip(k), px, core)))
    sends.append(copy(g_in, recv_g.at[core], gs.at[0], gr.at[core], partner))
    for k in (0, 1, 3, 2):
        for e in (0, 1):
            if k == 0 and e == 0:
                continue
            c = lax.rem(core + e, 2)
            slot = 2 * k + core
            sends.append(copy(send_x.at[slice_of(to_chip(k), c)], recv_x.at[slot], xs.at[2 * k + e], xr.at[slot],
                              at(pz, to_chip(k), px, c)))
    signal(across, at(pz, y + 4, px, core))
    for send in sends:
        send.start()
    recv_x[core] = send_x[shard]
    recv_g[core] = g_in[...]

    sortmt[...] = one_hot(sort_target(col) == row)
    ri, rj, rk = (row >> 4) & 3, (row >> 2) & 3, row & 3
    ci, cj, ck = (col >> 4) & 3, (col >> 2) & 3, col & 3
    for n, (si, sj, sk) in enumerate(COMBOS):
        if n == 0:
            continue
        step = 16 * si + 4 * sj + sk
        ok = (col == row + step) & (ri >= -si) & (rj >= -sj) & (rk >= -sk)
        shiftm[n] = one_hot(ok)
        ok = (row == col + step) & (ci >= -si) & (cj >= -sj) & (ck >= -sk)
        shiftmt[n] = one_hot(ok)
    wf[...] = jnp.zeros_like(wf)
    wcat[...] = jnp.zeros_like(wcat)
    w27[...] = jnp.zeros_like(w27)
    loads[2].wait()
    for n in range(8):
        first, width = lane_of(n)
        for par, parity in enumerate(PARITIES):
            tap = tap_of(n, parity)
            if tap is None:
                continue
            at_row = first + par * 32 - (256 - width)
            wf[at_row:at_row + 32, :] = w_in[tap]
            wcat[par * 32:par * 32 + 32, n * 256:n * 256 + 256] = w_in[tap]
    first = lane_of(DIRECT)[0]
    wf[first:first + 32, :] = w_in[27]
    w27[0:32, :] = w_in[27]

    def arrived(buf, sem, slot):
        copy(buf.at[slot], buf.at[slot], xs.at[0], sem.at[slot], partner).wait_recv()

    for k in (1, 2, 3):
        slot = 2 * k + core
        arrived(recv_g, gr, slot)
        sends.append(copy(recv_g.at[slot], recv_g.at[slot], fs.at[k], gr.at[slot], partner))
        sends[-1].start()

    for half in range(2):
        rows = slice(half * 256, half * 256 + 256)
        for k in (2 * half, 2 * half + 1):
            for e in (0, 1):
                if k or e:
                    arrived(recv_x, xr, 2 * k + lax.rem(core + e, 2))
        raw = recv_x[4 * half:4 * half + 4].reshape(256, 256)
        v = raw.astype(F32)
        s = 1.0 / (1.0 + jnp.exp(-v))
        act = (v * s).astype(BF16)
        dsilu[rows, :] = s * (1.0 + v * (1.0 - s))
        cols[rows, 0:256] = act
        lane = lax.broadcasted_iota(jnp.int32, (256, 256), 1)
        for n in range(1, 8):
            first, width = lane_of(n)
            moved = dot(shiftm[n], act[:, 256 - width:], NN)
            if n == DIRECT:
                moved = jnp.where(lane < 32, v, moved)
            cols[rows, first:first + width] = moved.astype(BF16)
        for k in (2 * half, 2 * half + 1):
            arrived(recv_g, gr, 2 * k + 1 - core)
        if half == 0:
            four = recv_g[0:4].reshape(256, 256)
            for block in range(6):
                acc[block * 256:block * 256 + 256, :] = dot(cols[0:256, block * 256:block * 256 + 256], four, TN)


    grads = recv_g[...].reshape(512, 256)
    for block in range(6):
        got = dot(cols[256:, block * 256:block * 256 + 256], grads[256:], TN)
        got = (got + acc[block * 256:block * 256 + 256, :]).astype(BF16)
        for n in range(8):
            first, width = lane_of(n)
            if first // 256 != block:
                continue
            for par, parity in enumerate(PARITIES):
                tap = tap_of(n, parity)
                if n == DIRECT and par == 0:
                    tap = 27
                if tap is None:
                    continue
                start = first + par * 32 - (256 - width) - block * 256
                place = (tap % taps_x) * 32
                gsend[tap // taps_x, place:place + 32, :] = got[start:start + 32, :]
    step1 = []
    for t, (_, y_, n) in enumerate(order()):
        for d in range(1, nx):
            other = lax.rem(px + d, nx)
            m = t * (nx - 1) + d - 1
            part = piece(y_ * ring + n)
            step1.append(copy(gsend.at[other, part], g1.at[d - 1, t], s1s.at[m], s1r.at[m], x_peer(d)))
            step1[-1].start()

    gcols[:, 0:256] = grads
    for half in range(2):
        rows = slice(half * 256, half * 256 + 256)
        for n in range(1, 8):
            gcols[rows, n * 256:n * 256 + 256] = dot(shiftmt[n], grads[rows, :], NN).astype(BF16)
    for half in range(2):
        rows = slice(half * 256, half * 256 + 256)
        got = dot(gcols[rows, :], wcat[...], NT) * dsilu[rows, :]
        direct = dot(grads[rows, :], w27[...], NT)
        for n in range(4):
            one = got[n * 64:n * 64 + 64, :]
            slot = 4 * half + n
            send_i[slot, :, 0:128] = (one[:, 0:128] + direct[n * 64:n * 64 + 64, :]).astype(BF16)
            send_i[slot, :, 128:256] = one[:, 128:256].astype(BF16)
        got = dot(cols[rows, :], wf[...], NN)
        for n in range(4):
            send_o[4 * half + n] = got[n * 64:n * 64 + 64, :].astype(BF16)
    home = []
    for k in (3, 1, 2, 0):
        for e in (0, 1):
            if k == 0 and e == 0:
                continue
            s = e if k else 1 - core
            chip = (y, y - 1, y + 1, y - far(e))[k]
            slot = 2 * k + s
            dev = at(pz, chip, px, s)
            n = 2 * k + e
            home.append(copy(send_i.at[slot], recv_i.at[shard], is_.at[n], ir.at[shard], dev))
            home.append(copy(send_o.at[slot], recv_o.at[shard], os_.at[n], or_.at[shard], dev))
    pl.semaphore_wait(across, 1)
    step2 = []
    for t, (own, y_, n) in enumerate(order()):
        for d in range(1, nx):
            step1[t * (nx - 1) + d - 1].wait()
        part = y_ * ring + n
        total = gsend[px, piece(part), :].astype(F32)
        for d in range(1, nx):
            total = total + g1[d - 1, t].astype(F32)
        s2[part] = total.astype(BF16)
        send = copy(s2.at[part], r2.at[q], s2s.at[t], s2r.at[q], owner(y_, n))
        if not own:
            send.start()
            step2.append(send)
        elif ring < nz:
            pl.when(pz == IDLE)(send.start)
            last2 = send
    r2[q] = s2[mine]

    recv_i[shard] = send_i[core]
    recv_o[shard] = send_o[core]

    def for_owners(body):
        if ring < nz:
            pl.when(is_owner)(body)
        else:
            body()

    part = piece(mine)
    step3 = [copy(fin.at[px, part], fin.at[px, part], s3s.at[t], s3r.at[q], owner(y_, n))
             for t, (own, y_, n) in enumerate(order()) if not own]
    if ring < nz:
        for n, y_ in enumerate((1 - y_hi, y_hi)):
            step3.append(copy(fin.at[px, part], fin.at[px, part], s3s.at[2 * ring + n], s3r.at[q],
                              at(IDLE, y_ * 4 + lax.rem(y, 4), px, core)))

    @for_owners
    def _():
        for d in range(1, nq):
            other = lax.rem(q + d, nq)
            copy(r2.at[other], r2.at[other], s2s.at[0], s2r.at[other], partner).wait_recv()
        fin[px, part, :] = jnp.sum(r2[...].astype(F32), axis=0).astype(BF16)
        for send in step3:
            send.start()

    for send in home:
        send.start()
    step4 = []
    places = list(order())[::-1]
    for t, (own, y_, n) in enumerate(places):
        theirs = piece(y_ * ring + n)
        sender = y_ * nz + (n + lax.div(n, IDLE) if ring < nz else n)
        come = copy(fin.at[px, theirs], fin.at[px, theirs], s3s.at[0], s3r.at[sender], partner)
        if not own:
            come.wait_recv()
        elif ring < nz:
            pl.when(pz == IDLE)(come.wait_recv)
        for d in range(1, nx):
            m = t * (nx - 1) + d - 1
            step4.append(copy(fin.at[px, theirs], fin.at[px, theirs], s4s.at[m], s4r.at[m], x_peer(d)))
            step4[-1].start()

    for e in range(1, 8):
        slot = lax.rem(shard + e, 8)
        for buf, ssem, sem in ((recv_i, is_, ir), (recv_o, os_, or_)):
            copy(buf.at[slot], buf.at[slot], ssem.at[0], sem.at[slot], at(pz, y, px, 1 - core)).wait_recv()
    out_v[...] = jnp.sum(recv_o[...].astype(F32), axis=0).astype(BF16)
    for par in range(8):
        for h in range(2):
            sorted_x[par, :, h * 128:h * 128 + 128] = jnp.concatenate(
                [recv_i[4 * h + n, :, par * 32:par * 32 + 32].astype(F32) for n in range(4)], axis=1)
    for b in range(2):
        natural = sorted_x[:, b * 32:b * 32 + 32, :].reshape(256, 256).astype(BF16)
        ig_v[b * 256:b * 256 + 256, :] = dot(sortmt[...], natural, NN).astype(BF16)

    for t, (own, y_, n) in enumerate(places):
        theirs = piece(y_ * ring + n)
        for d in range(1, nx):
            m = t * (nx - 1) + d - 1
            other = lax.rem(px + nx - d, nx)
            copy(fin.at[other, theirs], fin.at[other, theirs], s4s.at[m], s4r.at[m], x_peer(d)).wait_recv()
    for send in sends + home + step2 + step4:
        send.wait_send()
    if ring < nz:
        pl.when(pz == IDLE)(last2.wait_send)

    @for_owners
    def _():
        for send in step3:
            send.wait_send()


def finish(out_v, ig_v, fin, out_hbm, ig_hbm, wg_hbm, out_s, wg_s, sem):
    nx, rows = wg_s.shape[:2]
    stores = [pltpu.make_async_copy(ig_v, ig_hbm, sem.at[0])]
    stores[0].start()
    for n in range(nx):
        wg_s[n] = fin[n, 0:rows, :].astype(F32)
        stores.append(pltpu.make_async_copy(wg_s.at[n], wg_hbm.at[n], sem.at[n + 1]))
        stores[-1].start()
    out_s[...] = out_v[...].astype(F32).reshape(4, 4, 4, 256).astype(BF16)
    stores.append(pltpu.make_async_copy(out_s, out_hbm, sem.at[nx + 1]))
    stores[-1].start()
    for store in stores:
        store.wait()


def shards(nx, nz, inputs, cotangent, weights):
    nq = 2 * nz
    owners = 14 if nz == 8 else nq
    rows_x = 28 // nx * 32
    rows_q = rows_x // owners
    dma = pltpu.SemaphoreType.DMA
    sems = [dma((n,)) for n in (3, 8, 8, 4, 8, 4, 8, 8, 8, 8)]
    sems += [dma((max(n, 1),)) for n in (owners * (nx - 1), owners * (nx - 1), nq, nq, nq, nq, owners * (nx - 1), owners * (nx - 1))]
    sems += [pltpu.SemaphoreType.REGULAR]
    vm = pltpu.VMEM
    scratch = [
        vm((512, 256), BF16), vm((4, 4, 4, 256), BF16), vm((64, 256), BF16), vm((28, 32, 256), BF16),
        vm((256, 256), BF16), vm((256, 256), BF16), vm((8, 256, 256), BF16), vm((8, 256, 256), BF16),
        vm((8, 64, 256), F32), vm((8, 64, 256), BF16),
        vm((8, 64, 256), BF16), vm((8, 64, 256), BF16),
        vm((512, 1536), BF16), vm((512, 2048), BF16),
        vm((1536, 256), BF16), vm((256, 2048), BF16), vm((128, 256), BF16),
        vm((512, 256), F32), vm((1536, 256), F32),
        vm((8, 64, 256), BF16), vm((8, 64, 256), BF16),
        vm((8, 64, 256), BF16), vm((8, 64, 256), BF16),
        vm((nx, rows_x, 256), BF16), vm((max(nx - 1, 1), owners, rows_q, 256), BF16),
        vm((owners, rows_q, 256), BF16), vm((nq, rows_q, 256), BF16),
    ] + sems
    hbm = pl.BlockSpec(memory_space=pltpu.HBM)
    vmem = pl.BlockSpec(memory_space=pltpu.VMEM)
    out, ig, wg = pl.pallas_call(
        functools.partial(kernel, nx, nz),
        out_shape=(
            jax.ShapeDtypeStruct((64, 256), BF16),
            jax.ShapeDtypeStruct((512, 256), BF16),
            jax.ShapeDtypeStruct((nx, rows_x, 256), BF16),
        ),
        in_specs=[hbm] * 3,
        out_specs=(vmem,) * 3,
        scratch_shapes=scratch,
        compiler_params=pltpu.CompilerParams(
            collective_id=0, has_side_effects=True, vmem_limit_bytes=48 * 2**20),
        name="unit",
    )(*[pltpu.with_memory_space_constraint(a, pltpu.HBM)
        for a in (inputs.reshape(512, 256), cotangent.reshape(4, 4, 4, 256), weights)])
    out, ig, wg = pl.pallas_call(
        finish,
        out_shape=(
            jax.ShapeDtypeStruct((4, 4, 4, 256), BF16),
            jax.ShapeDtypeStruct((512, 256), BF16),
            jax.ShapeDtypeStruct((nx, rows_x, 256), F32),
        ),
        in_specs=[vmem] * 3,
        out_specs=(hbm,) * 3,
        scratch_shapes=[vm((4, 4, 4, 256), BF16), vm((nx, rows_x, 256), F32), dma((nx + 2,))],
        compiler_params=pltpu.CompilerParams(vmem_limit_bytes=8 * 2**20),
        name="finish",
    )(out, ig, wg)
    return (
        out.reshape(1, 4, 4, 4, 256),
        ig.reshape(1, 8, 8, 8, 256),
        wg.reshape(28, 32, 256),
    )


def solution(mesh, nx=4):
    nz = mesh.shape["dp"] // (2 * nx)
    rows = P(("dp", "shard"), None, None, None, None)
    return jax.shard_map(
        functools.partial(shards, nx, nz),
        mesh=mesh,
        in_specs=(rows, rows, P(None, "shard", None)),
        out_specs=(rows, rows, P(None, "shard", None)),
        check_vma=False,
    )
```

```python
import functools

import jax
import jax.numpy as jnp
from jax import lax
from jax.experimental import pallas as pl
from jax.experimental.pallas import tpu as pltpu
from jax.sharding import PartitionSpec as P

F32 = jnp.float32
BF16 = jnp.bfloat16
MESH = pl.DeviceIdType.MESH

COMBOS = [(si, sj, sk) for si in (0, -1) for sj in (0, -1) for sk in (0, -1)]
IDLE = 4
DIRECT = 2


def lane_of(combo):
    return (256 * combo, 256) if combo < 4 else (1024 + 128 * (combo - 4), 128)


def tap_of(combo, parity):
    total = 0
    for weight, shift, odd in zip((9, 3, 1), COMBOS[combo], parity):
        if shift and not odd:
            return None
        total += weight * (1 if not odd else 0 if shift else 2)
    return total


PARITIES = [(a, b, c) for a in (0, 1) for b in (0, 1) for c in (0, 1)]


def dot(a, b, dims):
    return lax.dot_general(a, b, (dims, ((), ())), preferred_element_type=F32)


NN = ((1,), (0,))
NT = ((1,), (1,))
TN = ((0,), (0,))


def one_hot(hit):
    return jnp.where(hit, 1.0, 0.0).astype(BF16)


def sort_target(rows):
    k, j, i = rows & 3, (rows >> 2) & 3, (rows >> 4) & 1
    pk, pj, pi = (rows >> 5) & 1, (rows >> 6) & 1, (rows >> 7) & 1
    return (2 * i + pi) * 64 + (2 * j + pj) * 8 + 2 * k + pk


def kernel(nx, nz, x_hbm, g_hbm, w_hbm, out_v, ig_v, fin,
           x_in, g_raw, g_in, w_in, sortm, sortmt, shiftm, shiftmt, sorted_x, send_x,
           recv_x, recv_g, cols, gcols, wf, wcat, w27, dsilu, acc, send_o, recv_o,
           send_i, recv_i, gsend, g1, s2, r2,
           in_sem, xs, xr, gs, gr, fs, os_, or_, is_, ir, s1s, s1r, s2s, s2r,
           s3s, s3r, s4s, s4r, across):
    nq = 2 * nz
    taps_x = 28 // nx
    rows_q = s2.shape[1]
    ring = s2.shape[0] // 2
    dp = lax.axis_index("dp")
    shard = lax.axis_index("shard")
    px = lax.rem(dp, nx)
    y_hi = lax.rem(lax.div(dp, nx), 2)
    pz = lax.div(dp, 2 * nx)
    y = y_hi * 4 + lax.div(shard, 2)
    core = lax.rem(shard, 2)
    sign = 1 - 2 * core
    q = y_hi * nz + pz

    def at(pz_, y_, px_, core_):
        y_ = lax.rem(y_ + 8, 8)
        return ((pz_ * 2 + lax.div(y_, 4)) * nx + px_, lax.rem(y_, 4) * 2 + core_)

    def slice_of(y_, core_):
        return lax.rem(y_ + 8, 4) * 2 + core_

    def x_peer(d):
        return at(pz, y, lax.rem(px + d, nx), core)

    def z_peer(d):
        return at(lax.rem(pz + d + nz, nz), y, px, core)

    here = lax.rem(pz - lax.div(pz, IDLE + 1), nz) if ring < nz else pz
    is_owner = pz != IDLE
    mine = y_hi * ring + here

    def owner(y_, n):
        return at(n + lax.div(n, IDLE) if ring < nz else n, y_ * 4 + lax.rem(y, 4), px, core)

    def order():
        offsets = sorted(range(ring), key=lambda e: -min(e, ring - e))
        for other_y in (1, 0):
            for e in offsets:
                y_ = 1 - y_hi if other_y else y_hi
                yield not other_y and e == 0, y_, lax.rem(here + e, ring)

    def piece(n):
        return pl.ds(pl.multiple_of(n * rows_q, 16), rows_q)

    partner = at(pz, y, px, 1 - core)

    def copy(src, dst, send, recv, dev):
        return pltpu.make_async_remote_copy(
            src_ref=src, dst_ref=dst, send_sem=send, recv_sem=recv, device_id=dev, device_id_type=MESH)

    def signal(sem, dev):
        pl.semaphore_signal(sem, inc=1, device_id=dev, device_id_type=MESH)

    loads = [pltpu.make_async_copy(a, b, in_sem.at[n]) for n, (a, b) in enumerate(((x_hbm, x_in), (g_hbm, g_raw), (w_hbm, w_in)))]
    for load in loads:
        load.start()

    peers = [partner]
    for d in (1, -1):
        for c in (0, 1):
            peers.append(at(pz, y + d, px, c))
    peers += [at(pz, y + 2 * sign, px, core), at(pz, y + 2 * sign, px, 1 - core), at(pz, y - 2 * sign, px, core)]
    peers += [x_peer(d) for d in range(1, nx)]
    peers += [z_peer(d) for d in range(1, nz)] + [at(pz, y + 4, px, core)]
    barrier = pltpu.get_barrier_semaphore()
    for peer in peers:
        signal(barrier, peer)

    row = lax.broadcasted_iota(jnp.int32, (256, 256), 0)
    col = lax.broadcasted_iota(jnp.int32, (256, 256), 1)
    sortm[...] = one_hot(sort_target(row) == col)
    loads[0].wait()
    for b in range(2):
        got = dot(sortm[...], x_in[b * 256:b * 256 + 256, :], NN)
        for par in range(8):
            sorted_x[par, b * 32:b * 32 + 32, :] = got[par * 32:par * 32 + 32, :]
    for p in range(8):
        for h in range(2):
            send_x[p, :, h * 128:h * 128 + 128] = jnp.concatenate(
                [sorted_x[4 * h + n, :, p * 32:p * 32 + 32] for n in range(4)], axis=1).astype(BF16)
    loads[1].wait()
    g_in[...] = g_raw[...].astype(F32).reshape(64, 256).astype(BF16)
    pl.semaphore_wait(barrier, len(peers))

    def far(c):
        return 2 - 4 * c

    def to_chip(k):
        return (y, y + 1, y - 1, y + 2 * sign)[k]

    sends = []
    for k in (3, 1, 2):
        slot = 2 * k + core
        sends.append(copy(g_in, recv_g.at[slot], gs.at[k], gr.at[slot], at(pz, to_chip(k), px, core)))
    sends.append(copy(g_in, recv_g.at[core], gs.at[0], gr.at[core], partner))
    for k in (0, 1, 3, 2):
        for e in (0, 1):
            if k == 0 and e == 0:
                continue
            c = lax.rem(core + e, 2)
            slot = 2 * k + core
            sends.append(copy(send_x.at[slice_of(to_chip(k), c)], recv_x.at[slot], xs.at[2 * k + e], xr.at[slot],
                              at(pz, to_chip(k), px, c)))
    signal(across, at(pz, y + 4, px, core))
    for send in sends:
        send.start()
    recv_x[core] = send_x[shard]
    recv_g[core] = g_in[...]

    sortmt[...] = one_hot(sort_target(col) == row)
    ri, rj, rk = (row >> 4) & 3, (row >> 2) & 3, row & 3
    ci, cj, ck = (col >> 4) & 3, (col >> 2) & 3, col & 3
    for n, (si, sj, sk) in enumerate(COMBOS):
        if n == 0:
            continue
        step = 16 * si + 4 * sj + sk
        ok = (col == row + step) & (ri >= -si) & (rj >= -sj) & (rk >= -sk)
        shiftm[n] = one_hot(ok)
        ok = (row == col + step) & (ci >= -si) & (cj >= -sj) & (ck >= -sk)
        shiftmt[n] = one_hot(ok)
    wf[...] = jnp.zeros_like(wf)
    wcat[...] = jnp.zeros_like(wcat)
    w27[...] = jnp.zeros_like(w27)
    loads[2].wait()
    for n in range(8):
        first, width = lane_of(n)
        for par, parity in enumerate(PARITIES):
            tap = tap_of(n, parity)
            if tap is None:
                continue
            at_row = first + par * 32 - (256 - width)
            wf[at_row:at_row + 32, :] = w_in[tap]
            wcat[par * 32:par * 32 + 32, n * 256:n * 256 + 256] = w_in[tap]
    first = lane_of(DIRECT)[0]
    wf[first:first + 32, :] = w_in[27]
    w27[0:32, :] = w_in[27]

    def arrived(buf, sem, slot):
        copy(buf.at[slot], buf.at[slot], xs.at[0], sem.at[slot], partner).wait_recv()

    for k in (1, 2, 3):
        slot = 2 * k + core
        arrived(recv_g, gr, slot)
        sends.append(copy(recv_g.at[slot], recv_g.at[slot], fs.at[k], gr.at[slot], partner))
        sends[-1].start()

    for half in range(2):
        rows = slice(half * 256, half * 256 + 256)
        for k in (2 * half, 2 * half + 1):
            for e in (0, 1):
                if k or e:
                    arrived(recv_x, xr, 2 * k + lax.rem(core + e, 2))
        raw = recv_x[4 * half:4 * half + 4].reshape(256, 256)
        v = raw.astype(F32)
        s = 1.0 / (1.0 + jnp.exp(-v))
        act = (v * s).astype(BF16)
        dsilu[rows, :] = s * (1.0 + v * (1.0 - s))
        cols[rows, 0:256] = act
        lane = lax.broadcasted_iota(jnp.int32, (256, 256), 1)
        for n in range(1, 8):
            first, width = lane_of(n)
            moved = dot(shiftm[n], act[:, 256 - width:], NN)
            if n == DIRECT:
                moved = jnp.where(lane < 32, v, moved)
            cols[rows, first:first + width] = moved.astype(BF16)
        for k in (2 * half, 2 * half + 1):
            arrived(recv_g, gr, 2 * k + 1 - core)
        if half == 0:
            four = recv_g[0:4].reshape(256, 256)
            for block in range(6):
                acc[block * 256:block * 256 + 256, :] = dot(cols[0:256, block * 256:block * 256 + 256], four, TN)


    grads = recv_g[...].reshape(512, 256)
    for block in range(6):
        got = dot(cols[256:, block * 256:block * 256 + 256], grads[256:], TN)
        got = (got + acc[block * 256:block * 256 + 256, :]).astype(BF16)
        for n in range(8):
            first, width = lane_of(n)
            if first // 256 != block:
                continue
            for par, parity in enumerate(PARITIES):
                tap = tap_of(n, parity)
                if n == DIRECT and par == 0:
                    tap = 27
                if tap is None:
                    continue
                start = first + par * 32 - (256 - width) - block * 256
                place = (tap % taps_x) * 32
                gsend[tap // taps_x, place:place + 32, :] = got[start:start + 32, :]
    step1 = []
    for t, (_, y_, n) in enumerate(order()):
        for d in range(1, nx):
            other = lax.rem(px + d, nx)
            m = t * (nx - 1) + d - 1
            part = piece(y_ * ring + n)
            step1.append(copy(gsend.at[other, part], g1.at[d - 1, t], s1s.at[m], s1r.at[m], x_peer(d)))
            step1[-1].start()

    gcols[:, 0:256] = grads
    for half in range(2):
        rows = slice(half * 256, half * 256 + 256)
        for n in range(1, 8):
            gcols[rows, n * 256:n * 256 + 256] = dot(shiftmt[n], grads[rows, :], NN).astype(BF16)
    for half in range(2):
        rows = slice(half * 256, half * 256 + 256)
        got = dot(gcols[rows, :], wcat[...], NT) * dsilu[rows, :]
        direct = dot(grads[rows, :], w27[...], NT)
        for n in range(4):
            one = got[n * 64:n * 64 + 64, :]
            slot = 4 * half + n
            send_i[slot, :, 0:128] = (one[:, 0:128] + direct[n * 64:n * 64 + 64, :]).astype(BF16)
            send_i[slot, :, 128:256] = one[:, 128:256].astype(BF16)
        got = dot(cols[rows, :], wf[...], NN)
        for n in range(4):
            send_o[4 * half + n] = got[n * 64:n * 64 + 64, :].astype(BF16)
    home = []
    for k in (3, 1, 2, 0):
        for e in (0, 1):
            if k == 0 and e == 0:
                continue
            s = e if k else 1 - core
            chip = (y, y - 1, y + 1, y - far(e))[k]
            slot = 2 * k + s
            dev = at(pz, chip, px, s)
            n = 2 * k + e
            home.append(copy(send_i.at[slot], recv_i.at[shard], is_.at[n], ir.at[shard], dev))
            home.append(copy(send_o.at[slot], recv_o.at[shard], os_.at[n], or_.at[shard], dev))
    pl.semaphore_wait(across, 1)
    step2 = []
    for t, (own, y_, n) in enumerate(order()):
        for d in range(1, nx):
            step1[t * (nx - 1) + d - 1].wait_recv()
        part = y_ * ring + n
        total = gsend[px, piece(part), :].astype(F32)
        for d in range(1, nx):
            total = total + g1[d - 1, t].astype(F32)
        s2[part] = total.astype(BF16)
        send = copy(s2.at[part], r2.at[q], s2s.at[t], s2r.at[q], owner(y_, n))
        if not own:
            send.start()
            step2.append(send)
        elif ring < nz:
            pl.when(pz == IDLE)(send.start)
            last2 = send
    r2[q] = s2[mine]

    recv_i[shard] = send_i[core]
    recv_o[shard] = send_o[core]

    def for_owners(body):
        if ring < nz:
            pl.when(is_owner)(body)
        else:
            body()

    part = piece(mine)
    step3 = [copy(fin.at[px, part], fin.at[px, part], s3s.at[t], s3r.at[q], owner(y_, n))
             for t, (own, y_, n) in enumerate(order()) if not own]
    if ring < nz:
        for n, y_ in enumerate((1 - y_hi, y_hi)):
            step3.append(copy(fin.at[px, part], fin.at[px, part], s3s.at[2 * ring + n], s3r.at[q],
                              at(IDLE, y_ * 4 + lax.rem(y, 4), px, core)))

    @for_owners
    def _():
        for d in range(1, nq):
            other = lax.rem(q + d, nq)
            copy(r2.at[other], r2.at[other], s2s.at[0], s2r.at[other], partner).wait_recv()
        fin[px, part, :] = jnp.sum(r2[...].astype(F32), axis=0).astype(BF16)
        for send in step3:
            send.start()

    for send in home:
        send.start()
    step4 = []
    places = list(order())[::-1]
    for t, (own, y_, n) in enumerate(places):
        theirs = piece(y_ * ring + n)
        sender = y_ * nz + (n + lax.div(n, IDLE) if ring < nz else n)
        come = copy(fin.at[px, theirs], fin.at[px, theirs], s3s.at[0], s3r.at[sender], partner)
        if not own:
            come.wait_recv()
        elif ring < nz:
            pl.when(pz == IDLE)(come.wait_recv)
        for d in range(1, nx):
            m = t * (nx - 1) + d - 1
            step4.append(copy(fin.at[px, theirs], fin.at[px, theirs], s4s.at[m], s4r.at[m], x_peer(d)))
            step4[-1].start()

    for e in range(1, 8):
        slot = lax.rem(shard + e, 8)
        for buf, ssem, sem in ((recv_i, is_, ir), (recv_o, os_, or_)):
            copy(buf.at[slot], buf.at[slot], ssem.at[0], sem.at[slot], at(pz, y, px, 1 - core)).wait_recv()
    out_v[...] = jnp.sum(recv_o[...].astype(F32), axis=0).astype(BF16)
    for par in range(8):
        for h in range(2):
            sorted_x[par, :, h * 128:h * 128 + 128] = jnp.concatenate(
                [recv_i[4 * h + n, :, par * 32:par * 32 + 32].astype(F32) for n in range(4)], axis=1)
    for b in range(2):
        natural = sorted_x[:, b * 32:b * 32 + 32, :].reshape(256, 256).astype(BF16)
        ig_v[b * 256:b * 256 + 256, :] = dot(sortmt[...], natural, NN).astype(BF16)

    for t, (own, y_, n) in enumerate(places):
        theirs = piece(y_ * ring + n)
        for d in range(1, nx):
            m = t * (nx - 1) + d - 1
            other = lax.rem(px + nx - d, nx)
            copy(fin.at[other, theirs], fin.at[other, theirs], s4s.at[m], s4r.at[m], x_peer(d)).wait_recv()
    for send in sends + step1 + home + step2 + step4:
        send.wait_send()
    if ring < nz:
        pl.when(pz == IDLE)(last2.wait_send)

    @for_owners
    def _():
        for send in step3:
            send.wait_send()


def finish(out_v, ig_v, fin, out_hbm, ig_hbm, wg_hbm, out_s, wg_s, sem):
    nx, rows = wg_s.shape[:2]
    stores = [pltpu.make_async_copy(ig_v, ig_hbm, sem.at[0])]
    stores[0].start()
    for n in range(nx):
        wg_s[n] = fin[n, 0:rows, :].astype(F32)
        stores.append(pltpu.make_async_copy(wg_s.at[n], wg_hbm.at[n], sem.at[n + 1]))
        stores[-1].start()
    out_s[...] = out_v[...].astype(F32).reshape(4, 4, 4, 256).astype(BF16)
    stores.append(pltpu.make_async_copy(out_s, out_hbm, sem.at[nx + 1]))
    stores[-1].start()
    for store in stores:
        store.wait()


def shards(nx, nz, inputs, cotangent, weights):
    nq = 2 * nz
    owners = 14 if nz == 8 else nq
    rows_x = 28 // nx * 32
    rows_q = rows_x // owners
    dma = pltpu.SemaphoreType.DMA
    sems = [dma((n,)) for n in (3, 8, 8, 4, 8, 4, 8, 8, 8, 8)]
    sems += [dma((max(n, 1),)) for n in (owners * (nx - 1), owners * (nx - 1), nq, nq, nq, nq, owners * (nx - 1), owners * (nx - 1))]
    sems += [pltpu.SemaphoreType.REGULAR]
    vm = pltpu.VMEM
    scratch = [
        vm((512, 256), BF16), vm((4, 4, 4, 256), BF16), vm((64, 256), BF16), vm((28, 32, 256), BF16),
        vm((256, 256), BF16), vm((256, 256), BF16), vm((8, 256, 256), BF16), vm((8, 256, 256), BF16),
        vm((8, 64, 256), F32), vm((8, 64, 256), BF16),
        vm((8, 64, 256), BF16), vm((8, 64, 256), BF16),
        vm((512, 1536), BF16), vm((512, 2048), BF16),
        vm((1536, 256), BF16), vm((256, 2048), BF16), vm((128, 256), BF16),
        vm((512, 256), F32), vm((1536, 256), F32),
        vm((8, 64, 256), BF16), vm((8, 64, 256), BF16),
        vm((8, 64, 256), BF16), vm((8, 64, 256), BF16),
        vm((nx, rows_x, 256), BF16), vm((max(nx - 1, 1), owners, rows_q, 256), BF16),
        vm((owners, rows_q, 256), BF16), vm((nq, rows_q, 256), BF16),
    ] + sems
    hbm = pl.BlockSpec(memory_space=pltpu.HBM)
    vmem = pl.BlockSpec(memory_space=pltpu.VMEM)
    out, ig, wg = pl.pallas_call(
        functools.partial(kernel, nx, nz),
        out_shape=(
            jax.ShapeDtypeStruct((64, 256), BF16),
            jax.ShapeDtypeStruct((512, 256), BF16),
            jax.ShapeDtypeStruct((nx, rows_x, 256), BF16),
        ),
        in_specs=[hbm] * 3,
        out_specs=(vmem,) * 3,
        scratch_shapes=scratch,
        compiler_params=pltpu.CompilerParams(
            collective_id=0, has_side_effects=True, vmem_limit_bytes=48 * 2**20),
        name="unit",
    )(*[pltpu.with_memory_space_constraint(a, pltpu.HBM)
        for a in (inputs.reshape(512, 256), cotangent.reshape(4, 4, 4, 256), weights)])
    out, ig, wg = pl.pallas_call(
        finish,
        out_shape=(
            jax.ShapeDtypeStruct((4, 4, 4, 256), BF16),
            jax.ShapeDtypeStruct((512, 256), BF16),
            jax.ShapeDtypeStruct((nx, rows_x, 256), F32),
        ),
        in_specs=[vmem] * 3,
        out_specs=(hbm,) * 3,
        scratch_shapes=[vm((4, 4, 4, 256), BF16), vm((nx, rows_x, 256), F32), dma((nx + 2,))],
        compiler_params=pltpu.CompilerParams(vmem_limit_bytes=8 * 2**20),
        name="finish",
    )(out, ig, wg)
    return (
        out.reshape(1, 4, 4, 4, 256),
        ig.reshape(1, 8, 8, 8, 256),
        wg.reshape(28, 32, 256),
    )


def solution(mesh, nx=4):
    nz = mesh.shape["dp"] // (2 * nx)
    rows = P(("dp", "shard"), None, None, None, None)
    return jax.shard_map(
        functools.partial(shards, nx, nz),
        mesh=mesh,
        in_specs=(rows, rows, P(None, "shard", None)),
        out_specs=(rows, rows, P(None, "shard", None)),
        check_vma=False,
    )
```
